128 devices in a mesh: agent: 2 (over x_hi), row: 8 (over x_lo, z), col: 8 (over y, core).
Axes of the slice: x: 4 (x_hi: 2, x_lo: 2; x = x_hi * 2 + x_lo), y: 4, z: 4, core: 2. Of those that a mesh axis runs over, the one named last changes fastest.
Arguments:
- probe_field: float32 [2, 256, 256], replicated, may hold values from -4.2 to 4.2
- offsets: int32 [2, 32, 16], P(None, ('agent', 'row'), 'col'), may hold values from -32 to 32
- amplitudes: float32 [32, 16, 256, 256], P(('agent', 'row'), 'col'), may hold values from 0.2 to 2
- data_state: float32 [2, 2048, 1024], P(None, ('agent', 'row'), 'col'), may hold values from -4.2 to 4.2
- prior_state: float32 [2, 2048, 1024], P(None, ('agent', 'row', 'col')), may hold values from -4.2 to 4.2
- first_weights: bfloat16 [3, 32, 6], replicated, may hold values from -2 to 2
- middle_weights: bfloat16 [4, 3, 32, 96], replicated, may hold values from -0.5 to 0.5
- last_weights: bfloat16 [3, 2, 96], replicated, may hold values from -0.375 to 0.375
Outputs:
- data_next: float32 [2, 2048, 1024], P(None, ('agent', 'row'), 'col')
- prior_next: float32 [2, 2048, 1024], P(None, ('agent', 'row', 'col'))
The draws below stay inside these ranges and needn't reach their ends.
All inputs are finite; a program needn't handle non-finite values.
Results may differ from the reference program's by a relative error of at most 0.0073.
Values may be sent and summed in bfloat16 or wider, within the bound.
A program may use at most 64 MiB of HBM per device.

```python
import math
import jax
import jax.numpy as jnp
from jax import lax

TILE_ROWS = 128
PROBE = 256
STEP = 64
JITTER = 32
CH = 32
LAYERS = 6
HALO = 128
HEIGHT = 2048
WIDTH = 1024
POS_ROWS = 32
POS_COLS = 16


def plant(entries, key, least, high):
    longest = entries.shape.index(max(entries.shape))
    spots = []
    for shift in (0, 1):
        where = [jax.random.randint(jax.random.fold_in(key, axis), (), 0, length) for axis, length in enumerate(entries.shape)]
        where[longest] = (where[longest] + shift) % entries.shape[longest]
        spots.append(tuple(where))
    return entries.at[spots[0]].set(least).at[spots[1]].set(high)


def level_of(own_key, dims, cuts, smallest, high):
    def one(axis_at, shards_of):
        draws = jax.random.uniform(jax.random.fold_in(jax.random.fold_in(own_key, 6), axis_at), (shards_of,), jnp.float32, smallest / len(cuts), high / len(cuts))
        return jnp.repeat(jnp.exp(draws), dims[axis_at] // shards_of).reshape((-1,) + (1,) * (len(dims) - axis_at - 1))

    loudness = one(*cuts[0])
    for cut in cuts[1:]:
        loudness = loudness * one(*cut)
    return loudness


def gaussian(rng, dims, width, reach, shards=(), kind=jnp.bfloat16):
    values = width * jax.random.normal(rng, dims, jnp.float32)
    if shards:
        values = values * level_of(rng, dims, shards, -0.22, 0.18)
    return jnp.clip(values, -reach, reach).astype(kind)


def setup_inputs(seed: int = 0) -> dict:
    key_of = jax.random.split(jax.random.key(seed), 9)
    probe_field = gaussian(key_of[0], (2, PROBE, PROBE), 0.7, 4.2, (), jnp.float32)
    offsets = plant(jax.random.randint(key_of[1], (2, POS_ROWS, POS_COLS), 0 - JITTER, JITTER + 1), jax.random.fold_in(key_of[1], 1), 0 - JITTER, JITTER).astype(jnp.int32)
    amplitudes = jnp.clip(0.2 + 1.8 * jax.random.uniform(key_of[2], (POS_ROWS, POS_COLS, PROBE, PROBE), jnp.float32) ** level_of(key_of[2], (POS_ROWS, POS_COLS, PROBE, PROBE), ((0, 16), (1, 8)), -0.2, 0.2), 0.2, 2.0)
    data_state = gaussian(key_of[3], (2, HEIGHT, WIDTH), 0.7, 4.2, ((1, 16), (2, 8)), jnp.float32)
    prior_state = gaussian(key_of[4], (2, HEIGHT, WIDTH), 0.7, 4.2, ((1, 128),), jnp.float32)
    first_weights = gaussian(key_of[5], (3, CH, 6), 9 ** -0.5, 2.0)
    middle_weights = gaussian(key_of[6], (LAYERS - 2, 3, CH, 3 * CH), (9 * CH // 2) ** -0.5, 0.5)
    last_weights = gaussian(key_of[7], (3, 2, 3 * CH), (9 * CH) ** -0.5, 0.375)
    return {"probe_field": probe_field, "offsets": offsets, "amplitudes": amplitudes, "data_state": data_state, "prior_state": prior_state, "first_weights": first_weights, "middle_weights": middle_weights, "last_weights": last_weights}


MAGNITUDE_FLOOR = 0.5
DATA_STEP = 0.125
DATA_WEIGHT = 0.6
RELAXATION = 0.5

def as_index(value):
    return jnp.asarray(value).astype(jnp.int32)

def dft_tables():
    numbers = jnp.arange(PROBE, dtype=jnp.int32)
    product = numbers[:, None] * numbers[None, :] % PROBE
    angles = product.astype(jnp.float32) * (2.0 * math.pi / PROBE)
    scaling = 1.0 / math.sqrt(PROBE)
    return ((jnp.cos(angles) * scaling).astype(jnp.bfloat16), (-jnp.sin(angles) * scaling).astype(jnp.bfloat16))

def right_product(left_real, left_imag, table_real, table_imag):
    joined = jnp.concatenate([left_real, left_imag], axis=-1).astype(jnp.float32)
    table = jnp.concatenate([jnp.concatenate([table_real, table_imag], axis=1), jnp.concatenate([-table_imag, table_real], axis=1)], axis=0).astype(jnp.float32)
    output = jnp.einsum('bjk,kw->bjw', joined, table)
    midpoint = left_real.shape[-1]
    return (output[..., :midpoint], output[..., midpoint:])

def left_product(table_real, table_imag, right_real, right_imag):
    stacked = jnp.concatenate([table_real, table_imag], axis=0).astype(jnp.float32)
    first = jnp.einsum('jk,bkw->bjw', stacked, right_real.astype(jnp.float32))
    second = jnp.einsum('jk,bkw->bjw', stacked, right_imag.astype(jnp.float32))
    midpoint = table_real.shape[0]
    return (first[:, :midpoint] - second[:, midpoint:], first[:, midpoint:] + second[:, :midpoint])

def position_terms(patches, measured, probe_field, table_real, table_imag):
    probe_real = probe_field[0]
    probe_imag = probe_field[1]
    object_real = patches[:, 0]
    object_imag = patches[:, 1]
    exit_real = (probe_real * object_real - probe_imag * object_imag).astype(jnp.bfloat16)
    exit_imag = (probe_real * object_imag + probe_imag * object_real).astype(jnp.bfloat16)
    half_real, half_imag = right_product(exit_real, exit_imag, table_real, table_imag)
    wave_real, wave_imag = left_product(table_real, table_imag, half_real.astype(jnp.bfloat16), half_imag.astype(jnp.bfloat16))
    magnitude = jnp.sqrt(wave_real * wave_real + wave_imag * wave_imag)
    retained = 1.0 - measured / jnp.maximum(magnitude, MAGNITUDE_FLOOR)
    resid_real = (wave_real * retained).astype(jnp.bfloat16)
    resid_imag = (wave_imag * retained).astype(jnp.bfloat16)
    back_real, back_imag = right_product(resid_real, resid_imag, table_real, -table_imag)
    field_real, field_imag = left_product(table_real, -table_imag, back_real.astype(jnp.bfloat16), back_imag.astype(jnp.bfloat16))
    contrib_real = probe_real * field_real + probe_imag * field_imag
    contrib_imag = probe_real * field_imag - probe_imag * field_real
    return jnp.stack([contrib_real, contrib_imag], axis=1)

def convolve(current, weight):
    row_count = current.shape[1] - 2
    col_count = current.shape[2]
    widened = jnp.pad(current, ((0, 0), (0, 0), (1, 1)))
    summed = None
    for shift_row in range(3):
        stacked = jnp.concatenate([widened[:, shift_row:shift_row + row_count, shift_col:shift_col + col_count] for shift_col in range(3)], axis=0)
        contribution = jnp.einsum('ok,krw->orw', weight[shift_row].astype(jnp.float32), stacked.astype(jnp.float32))
        summed = contribution if summed is None else summed + contribution
    return summed

def denoise_rows(current, first_row, height, weights):
    output = None
    for depth in range(LAYERS):
        output = convolve(current, weights[depth])
        first_row = first_row + 1
        if depth < LAYERS - 1:
            row_ids = first_row + jnp.arange(output.shape[1], dtype=jnp.int32)
            inside = (row_ids >= 0) & (row_ids < height)
            current = jnp.where(inside[None, :, None], jax.nn.relu(output), 0.0).astype(jnp.bfloat16)
    return output

def reference(probe_field, offsets, amplitudes, data_state, prior_state, first_weights, middle_weights, last_weights):
    table_real, table_imag = dft_tables()
    padded = jnp.pad(data_state, ((0, 0), (HALO, HALO), (HALO, HALO)))
    col_base = jnp.arange(POS_COLS, dtype=jnp.int32) * STEP + JITTER
    anchor_zero = as_index(0)

    def row_pass(buffer, inputs):
        number, shifts, measured = inputs
        upper_edges = as_index(number * STEP + JITTER + shifts[0])
        left_edges = as_index(col_base + shifts[1])
        patches = jax.vmap(lambda upper_edge, left_edge: lax.dynamic_slice(padded, (anchor_zero, as_index(upper_edge), as_index(left_edge)), (2, PROBE, PROBE)))(upper_edges, left_edges)
        contributions = position_terms(patches, measured, probe_field, table_real, table_imag)

        def scatter_one(position, accumulator):
            upper_edge = as_index(upper_edges[position])
            left_edge = as_index(left_edges[position])
            current = lax.dynamic_slice(accumulator, (anchor_zero, upper_edge, left_edge), (2, PROBE, PROBE))
            return lax.dynamic_update_slice(accumulator, current + contributions[position], (anchor_zero, upper_edge, left_edge))
        return (lax.fori_loop(0, POS_COLS, scatter_one, buffer), None)
    scanned = lax.scan(row_pass, jnp.zeros(padded.shape, jnp.float32), (jnp.arange(POS_ROWS, dtype=jnp.int32), jnp.moveaxis(offsets, 1, 0).astype(jnp.int32), amplitudes))
    gradient = scanned[0][:, HALO:HALO + HEIGHT, HALO:HALO + WIDTH]
    data_update = data_state - DATA_STEP * gradient
    data_reflect = 2.0 * data_update - data_state
    weights = [first_weights] + [middle_weights[number] for number in range(LAYERS - 2)] + [last_weights]
    inputs = jnp.pad(prior_state.astype(jnp.bfloat16), ((0, 0), (LAYERS, LAYERS), (0, 0)))

    def block_pass(number):
        anchor = as_index(number * TILE_ROWS)
        window = lax.dynamic_slice(inputs, (anchor_zero, anchor, anchor_zero), (2, TILE_ROWS + 2 * LAYERS, WIDTH))
        return denoise_rows(window, anchor - LAYERS, HEIGHT, weights)
    blocks = lax.map(block_pass, jnp.arange(HEIGHT // TILE_ROWS, dtype=jnp.int32))
    noise = jnp.moveaxis(blocks, 0, 1).reshape(2, HEIGHT, WIDTH)
    prior_update = prior_state - noise
    prior_reflect = 2.0 * prior_update - prior_state
    consensus = DATA_WEIGHT * data_reflect + (1.0 - DATA_WEIGHT) * prior_reflect
    data_next = (1.0 - RELAXATION) * data_state + RELAXATION * (2.0 * consensus - data_reflect)
    prior_next = (1.0 - RELAXATION) * prior_state + RELAXATION * (2.0 * consensus - prior_reflect)
    return (data_next, prior_next)
```

```python
import functools
import math

import jax
import jax.numpy as jnp
import numpy as np
from jax import lax
from jax.experimental import pallas as pl
from jax.experimental.pallas import tpu as pltpu
from jax.sharding import PartitionSpec as P

PROBE = 256
STEP = 64
JITTER = 32
TILE = 128
STRIP = 16
LAYERS = 6
EXT = 384
QUADS = 256
PAIRS = 13
POSITIONS = 4

BF = jnp.bfloat16
F32 = jnp.float32
MESH = pl.DeviceIdType.MESH


def fourier_table():
    numbers = np.arange(PROBE)
    product = (numbers[:, None] * numbers[None, :]) % PROBE
    angles = product * (2.0 * math.pi / PROBE)
    scaling = 1.0 / math.sqrt(PROBE)
    return np.stack([np.cos(angles) * scaling, -np.sin(angles) * scaling]).astype(np.float32)


def dot(left, right):
    return lax.dot_general(left, right, (((1,), (0,)), ((), ())), preferred_element_type=F32)


def dot_nt(left, right):
    return lax.dot_general(left, right, (((1,), (1,)), ((), ())), preferred_element_type=F32)


def slot_of(row, column):
    return column ^ 1 if row else column


def center_lane(row, column):
    return (row // 2) * 256 + (row % 2) * 128 + slot_of(row % 2, column) * 32


def edge_lane(row, column):
    odd = row % 2
    slot = (1 if odd else 0) if column == 4 else (2 if odd else 3)
    return 512 + (row // 2) * 128 + slot * 32


def input_lane(row, column):
    return center_lane(row, column) if 0 <= column < 4 else edge_lane(row, column)


def kernel(
    offsets,
    probe_any,
    amps_any,
    ds_ref,
    ps_any,
    first_ref,
    middle_ref,
    last_ref,
    table_ref,
    data_out,
    prior_out,
    probe,
    amps,
    xf,
    obh,
    obl,
    obr,
    obj,
    acc,
    ff,
    gg,
    ex,
    hs,
    wave,
    cp,
    gsend,
    grecv,
    rsend,
    rrecv,
    drb,
    drs,
    prb,
    prt,
    t1,
    t1r,
    tm,
    t6,
    t6b,
    d2,
    p2,
    xr,
    xv,
    xc,
    a0,
    a1,
    e0,
    e1,
    zz,
    osc,
    local_sem,
    halo_send,
    halo_recv,
    grad_send,
    grad_recv,
    dr_send,
    dr_recv,
    pr_send,
    pr_recv,
):
    agent, row, col = lax.axis_index("agent"), lax.axis_index("row"), lax.axis_index("col")
    tile_row = agent * 8 + row
    strip = tile_row * 8 + col

    def at(tile, column):
        return (lax.div(tile, 8), lax.rem(tile, 8), column)

    up = at(lax.rem(tile_row + 15, 16), col)
    down = at(lax.rem(tile_row + 1, 16), col)
    left = (agent, row, lax.rem(col + 7, 8))
    right = (agent, row, lax.rem(col + 1, 8))
    before, after = lax.rem(strip + 127, 128), lax.rem(strip + 1, 128)
    prev_strip = at(lax.div(before, 8), lax.rem(before, 8))
    next_strip = at(lax.div(after, 8), lax.rem(after, 8))
    peers = [lax.rem(col + k, 8) for k in range(1, 8)]

    def remote(src, dst, send, recv, device):
        return pltpu.make_async_remote_copy(
            src_ref=src, dst_ref=dst, send_sem=send, recv_sem=recv, device_id=device, device_id_type=MESH
        )

    own_strip = pltpu.make_async_copy(ps_any, xf.at[:, 8:24, :], local_sem.at[0])
    own_strip.start()
    load_probe = pltpu.make_async_copy(probe_any, probe, local_sem.at[1])
    load_probe.start()
    load_amps = pltpu.make_async_copy(amps_any, amps, local_sem.at[2])
    load_amps.start()

    barrier = pltpu.get_barrier_semaphore()
    greeted = [up, down, prev_strip, next_strip] + [(agent, row, c) for c in peers]
    for device in greeted:
        pl.semaphore_signal(barrier, inc=1, device_id=device, device_id_type=MESH)
    obh[:, 128:256, :] = ds_ref[...].astype(BF)
    pl.semaphore_wait(barrier, len(greeted))

    to_prev = remote(ps_any.at[:, 0:8, :], xf.at[:, 24:32, :], halo_send.at[0], halo_recv.at[0], prev_strip)
    to_next = remote(ps_any.at[:, 8:16, :], xf.at[:, 0:8, :], halo_send.at[1], halo_recv.at[1], next_strip)
    to_down = remote(obh.at[:, 128:256, :], obh.at[:, 0:128, :], halo_send.at[2], halo_recv.at[2], down)
    to_up = remote(obh.at[:, 128:256, :], obh.at[:, 256:384, :], halo_send.at[3], halo_recv.at[3], up)
    for copy in (to_prev, to_next, to_down, to_up):
        copy.start()

    tm[...] = jnp.zeros_like(tm)
    t6[...] = jnp.zeros_like(t6)
    for r in range(2):
        for c in range(4):
            at_row = r * 128 + slot_of(r, c) * 32
            for a in range(3):
                for b in range(3):
                    lane = input_lane(r + a, c + b - 1)
                    for layer in range(4):
                        tm[layer, at_row : at_row + 32, lane : lane + 32] = middle_ref[
                            layer, a, :, 32 * b : 32 * b + 32
                        ]
                    t6[r * 8 + c * 2 : r * 8 + c * 2 + 2, lane : lane + 32] = last_ref[
                        a, :, 32 * b : 32 * b + 32
                    ].astype(F32)
    t6b[...] = t6[...].astype(BF)

    lane_ids = lax.broadcasted_iota(jnp.int32, (32, 128), 1)
    firsts = [first_ref[a].astype(F32) for a in range(3)]
    for r in range(2):
        for c in range(4):
            at_row = r * 128 + slot_of(r, c) * 32
            parts = [jnp.zeros((32, 128), F32) for _ in range(3)]
            for a in range(3):
                for b in range(3):
                    column = c + b - 1
                    if 0 <= column < 4:
                        block, base = column // 2, (column % 2) * 64
                    else:
                        block, base = 2, 0 if column == 4 else 64
                    for k in range(2):
                        value = firsts[a][:, 2 * b + k : 2 * b + k + 1]
                        parts[block] = jnp.where(lane_ids == base + k * 32 + r + a, value, parts[block])
            for block in range(3):
                t1[at_row : at_row + 32, 128 * block : 128 * block + 128] = parts[block]

    def shift_first(pair, _):
        for block in range(3):
            t1r[pair, :, 128 * block : 128 * block + 128] = pltpu.roll(
                t1[:, 128 * block : 128 * block + 128], 2 + 2 * pair, 1
            ).astype(BF)
        return 0

    lax.fori_loop(0, PAIRS, shift_first, 0)

    vq = lax.broadcasted_iota(jnp.int32, (128, 512), 0)
    jc = lax.broadcasted_iota(jnp.int32, (128, 512), 1)
    hit = lax.rem(jc, 256) == 4 * lax.rem(vq, 64) + 2 * lax.div(vq, 64) + lax.div(jc, 256)
    d2[...] = jnp.where(hit, 1.0, 0.0).astype(BF)
    jq = lax.broadcasted_iota(jnp.int32, (512, 512), 0)
    cc = lax.broadcasted_iota(jnp.int32, (512, 512), 1)
    p2[...] = jnp.where(cc == 4 * lax.rem(jq, 128) + lax.div(jq, 128), 1.0, 0.0).astype(BF)

    real, imag = table_ref[0], table_ref[1]
    minus = (-imag.astype(F32)).astype(BF)
    ff[0:256, 0:256] = real
    ff[0:256, 256:512] = imag
    ff[256:512, 0:256] = minus
    ff[256:512, 256:512] = real
    gg[0:256, 0:256] = real
    gg[0:256, 256:512] = minus
    gg[256:512, 0:256] = imag
    gg[256:512, 256:512] = real

    own_strip.wait()
    to_prev.wait()
    to_next.wait()
    xr[...] = jnp.zeros_like(xr)
    zero_rows = jnp.zeros((8, 128), F32)
    for slot in range(2):
        xv[slot, 0:8, :] = zero_rows
        xv[slot, 264:272, :] = zero_rows
        zz[slot, 0:8, :] = zero_rows
        zz[slot, 264:272, :] = zero_rows
    keep_top = strip > 0
    keep_bottom = strip < 127
    for t in range(4):
        cols = slice(256 * t, 256 * t + 256)
        for k in range(2):
            piece = jnp.concatenate(
                [
                    jnp.where(keep_top, xf[k, 0:8, cols], 0.0),
                    xf[k, 8:24, cols],
                    jnp.where(keep_bottom, xf[k, 24:32, cols], 0.0),
                ],
                axis=0,
            ).astype(BF)
            xr[t, 32 * k : 32 * k + 32, 0:256] = piece
            xr[t, 64 + 32 * k : 96 + 32 * k, 256:512] = piece
        spread = dot_nt(d2[...], xr[t])
        xv[0, 8 + 64 * t : 72 + 64 * t, :] = spread[0:64]
        xv[1, 8 + 64 * t : 72 + 64 * t, :] = spread[64:128]
    wide_ids = lax.broadcasted_iota(jnp.int32, (QUADS, 128), 1)
    low_half = wide_ids < 64
    outer = (wide_ids < 32) | (wide_ids >= 96)
    xc[:, 0:128] = xv[0, 8:264, :].astype(BF)
    xc[:, 128:256] = xv[1, 8:264, :].astype(BF)
    xc[:, 256:384] = jnp.where(low_half, xv[0, 9:265, :], xv[1, 7:263, :]).astype(BF)

    to_down.wait()
    to_up.wait()
    to_right = remote(obh, obl, halo_send.at[4], halo_recv.at[4], right)
    to_left = remote(obh, obr, halo_send.at[5], halo_recv.at[5], left)
    to_right.start()
    to_left.start()

    def finish(y, first, pair, slot, a_out, e_out):
        top = first + 2 * pair
        in_top = (top >= 0) & (top < 2048)
        in_low = (top >= -1) & (top < 2047)
        y0 = jnp.where(in_top, jnp.maximum(y[:, 0:128], 0.0), 0.0)
        y1 = jnp.where(in_low, jnp.maximum(y[:, 128:256], 0.0), 0.0)
        a_out[pair, :, 0:128] = y0.astype(BF)
        a_out[pair, :, 128:256] = y1.astype(BF)
        zz[slot, 8:264, :] = jnp.where(outer, y0, y1)
        e_out[pair] = jnp.where(low_half, zz[slot, 9:265, :], zz[slot, 7:263, :]).astype(BF)

    base = strip * STRIP - LAYERS

    def first_layer(pair, _):
        finish(dot_nt(xc[...], t1r[pair]), base + 1, pair, 0, a0, e0)
        return 0

    lax.fori_loop(0, PAIRS, first_layer, 0)

    def window(a_in, e_in, pair):
        return jnp.concatenate([a_in[pair], a_in[pair + 1], e_in[pair], e_in[pair + 1]], axis=1)

    def middle_layer(depth, a_in, e_in, a_out, e_out):
        def body(pair, _):
            finish(dot_nt(window(a_in, e_in, pair), tm[depth - 2]), base + depth, pair, 0, a_out, e_out)
            return 0

        lax.fori_loop(0, PAIRS + 1 - depth, body, 0)

    middle_layer(2, a0, e0, a1, e1)

    to_right.wait()
    to_left.wait()
    load_probe.wait()
    load_amps.wait()
    for part in range(2):
        for block, source in enumerate((obl, obh, obr)):
            column_in = (col > 0, True, col < 7)[block]
            for third in range(3):
                rows = slice(128 * third, 128 * third + 128)
                if block == 1 and third == 1:
                    value = ds_ref[part]
                else:
                    inside = (tile_row > 0, True, tile_row < 15)[third]
                    keep = jnp.logical_and(inside, column_in)
                    value = jnp.where(keep, source[part, rows, :].astype(F32), 0.0)
                obj[part, block, rows, :] = value
    for part in range(2):
        for block in range(2):
            cp[part, block, 0:128, :] = jnp.zeros((128, 128), F32)
            cp[part, block, 384:512, :] = jnp.zeros((128, 128), F32)
        acc[part] = jnp.zeros((EXT, EXT), F32)

    def position(number, _):
        grid_row, grid_col = lax.div(number, 2), lax.rem(number, 2)
        upper = grid_row * STEP + JITTER + offsets[0, grid_row, grid_col]
        lefty = grid_col * STEP + JITTER + offsets[1, grid_row, grid_col]
        back_roll = lax.rem(EXT - lefty, EXT)
        for chunk in range(0, PROBE, 64):
            rows = slice(chunk, chunk + 64)
            o_r, o_i = [
                pltpu.roll(
                    jnp.concatenate(
                        [obj[part, block, pl.ds(upper + chunk, 64), :] for block in range(3)], axis=1
                    ),
                    back_roll,
                    1,
                )[:, 0:256]
                for part in range(2)
            ]
            p_r, p_i = probe[0, rows, :], probe[1, rows, :]
            ex[rows, 0:256] = (p_r * o_r - p_i * o_i).astype(BF)
            ex[rows, 256:512] = (p_r * o_i + p_i * o_r).astype(BF)
        hs[0:256, :] = dot(ex[...], ff[:, 0:256]).astype(BF)
        hs[256:512, :] = dot(ex[...], ff[:, 256:512]).astype(BF)
        wave[...] = dot(gg[...], hs[...])
        for chunk in range(0, PROBE, 64):
            rows = slice(chunk, chunk + 64)
            w_r, w_i = wave[rows, :], wave[256 + chunk : 320 + chunk, :]
            square = w_r * w_r + w_i * w_i
            retained = 1.0 - amps[number, rows, :] * lax.rsqrt(jnp.maximum(square, 0.25))
            ex[rows, 0:256] = (w_r * retained).astype(BF)
            ex[rows, 256:512] = (w_i * retained).astype(BF)
        hs[0:256, :] = dot(ex[...], gg[:, 0:256]).astype(BF)
        hs[256:512, :] = dot(ex[...], gg[:, 256:512]).astype(BF)
        wave[...] = dot(ff[...], hs[...])
        for chunk in range(0, PROBE, 64):
            rows = slice(chunk, chunk + 64)
            f_r, f_i = wave[rows, :], wave[256 + chunk : 320 + chunk, :]
            p_r, p_i = probe[0, rows, :], probe[1, rows, :]
            for part, term in enumerate((p_r * f_r + p_i * f_i, p_r * f_i - p_i * f_r)):
                for block in range(2):
                    cp[part, block, 128 + chunk : 192 + chunk, :] = term[:, 128 * block : 128 * block + 128]
        for part in range(2):
            for chunk in range(0, EXT, 64):
                term = [cp[part, block, pl.ds(128 - upper + chunk, 64), :] for block in range(2)]
                term = jnp.concatenate(term + [jnp.zeros((64, 128), F32)], axis=1)
                acc[part, chunk : chunk + 64, :] += pltpu.roll(term, lefty, 1)
        return 0

    lax.fori_loop(0, POSITIONS, position, 0)

    for part in range(2):
        gsend[0, part] = acc[part, :, 0:128].astype(BF)
        gsend[1, part] = acc[part, :, 256:384].astype(BF)
    grad_left = remote(gsend.at[0], grecv.at[1], grad_send.at[0], grad_recv.at[0], left)
    grad_right = remote(gsend.at[1], grecv.at[0], grad_send.at[1], grad_recv.at[1], right)
    grad_left.start()
    grad_right.start()

    middle_layer(3, a1, e1, a0, e0)

    grad_left.wait()
    grad_right.wait()
    keeps = (col > 0, col < 7)
    for part in range(2):
        total = acc[part, :, 128:256]
        for side in range(2):
            total = total + jnp.where(keeps[side], grecv[side, part].astype(F32), 0.0)
        acc[part, :, 128:256] = total
        rsend[0, part] = total[0:128].astype(BF)
        rsend[1, part] = total[256:384].astype(BF)
    grad_up = remote(rsend.at[0], rrecv.at[1], grad_send.at[2], grad_recv.at[2], up)
    grad_down = remote(rsend.at[1], rrecv.at[0], grad_send.at[3], grad_recv.at[3], down)
    grad_up.start()
    grad_down.start()

    middle_layer(4, a0, e0, a1, e1)

    grad_up.wait()
    grad_down.wait()
    keeps_row = (tile_row > 0, tile_row < 15)
    for part in range(2):
        total = acc[part, 128:256, 128:256]
        for side in range(2):
            total = total + jnp.where(keeps_row[side], rrecv[side, part].astype(F32), 0.0)
        reflect = ds_ref[part] - 0.25 * total
        acc[part, 128:256, 128:256] = reflect
        drb[part] = reflect.astype(BF)
    dr_copies = []
    for k, c in enumerate(peers):
        dr_copies.append(
            remote(
                drb.at[:, pl.ds(pl.multiple_of(c * STRIP, STRIP), STRIP), :],
                drs.at[col],
                dr_send.at[k],
                dr_recv.at[k],
                (agent, row, c),
            )
        )
        dr_copies[-1].start()
    drs[col] = drb[:, pl.ds(pl.multiple_of(col * STRIP, STRIP), STRIP), :]

    middle_layer(5, a1, e1, a0, e0)

    def last_layer(pair, _):
        y = dot_nt(t6b[...], window(a0, e0, pair))
        for r in range(2):
            for c in range(4):
                for k in range(2):
                    osc[c, pl.ds(k * STRIP + 2 * pair + r, 1), :] = y[r * 8 + c * 2 + k : r * 8 + c * 2 + k + 1, :]
        return 0

    lax.fori_loop(0, STRIP // 2, last_layer, 0)

    for half in range(2):
        joined = jnp.concatenate([osc[c, :, 128 * half : 128 * half + 128] for c in range(4)], axis=1)
        coarse = joined.astype(BF)
        fine = (joined - coarse.astype(F32)).astype(BF)
        both = dot(jnp.concatenate([coarse, fine], axis=0), p2[...])
        noise = both[0:32] + both[32:64]
        for k in range(2):
            cols = slice(512 * half, 512 * half + 512)
            reflect = xf[k, 8:24, cols] - 2.0 * noise[16 * k : 16 * k + 16]
            prior_out[k, :, cols] = 0.5 * xf[k, 8:24, cols] - 0.1 * reflect
            for c in range(4):
                prb[4 * half + c, k] = reflect[:, 128 * c : 128 * c + 128].astype(BF)
    pr_copies = []
    for k, c in enumerate(peers):
        pr_copies.append(remote(prb.at[c], prt.at[col], pr_send.at[k], pr_recv.at[k], (agent, row, c)))
        pr_copies[-1].start()
    prt[col] = prb[col]

    for copy in dr_copies:
        copy.wait()
    for c in range(8):
        cols = slice(128 * c, 128 * c + 128)
        for k in range(2):
            prior_out[k, :, cols] = prior_out[k, :, cols] + 0.6 * drs[c, k].astype(F32)
    for copy in pr_copies:
        copy.wait()
    for c in range(8):
        rows = slice(STRIP * c, STRIP * c + STRIP)
        for k in range(2):
            data_out[k, rows, :] = (
                0.5 * ds_ref[k, rows, :]
                + 0.1 * acc[k, 128 + STRIP * c : 144 + STRIP * c, 128:256]
                + 0.4 * prt[c, k].astype(F32)
            )


def on_device(
    probe_field, offsets, amplitudes, data_state, prior_state, first_weights, middle_weights, last_weights
):
    vmem = pl.BlockSpec(memory_space=pltpu.VMEM)
    anywhere = pl.BlockSpec(memory_space=pl.ANY)
    table = jnp.asarray(fourier_table()).astype(BF)
    dma = pltpu.SemaphoreType.DMA
    return pl.pallas_call(
        kernel,
        name="step",
        out_shape=(
            jax.ShapeDtypeStruct((2, TILE, TILE), F32),
            jax.ShapeDtypeStruct((2, STRIP, 1024), F32),
        ),
        in_specs=[
            pl.BlockSpec(memory_space=pltpu.SMEM),
            anywhere,
            anywhere,
            vmem,
            anywhere,
            vmem,
            vmem,
            vmem,
            vmem,
        ],
        out_specs=(vmem, vmem),
        scratch_shapes=[
            pltpu.VMEM((2, PROBE, PROBE), F32),
            pltpu.VMEM((POSITIONS, PROBE, PROBE), F32),
            pltpu.VMEM((2, 32, 1024), F32),
            pltpu.VMEM((2, EXT, TILE), BF),
            pltpu.VMEM((2, EXT, TILE), BF),
            pltpu.VMEM((2, EXT, TILE), BF),
            pltpu.VMEM((2, 3, EXT, TILE), F32),
            pltpu.VMEM((2, EXT, EXT), F32),
            pltpu.VMEM((512, 512), BF),
            pltpu.VMEM((512, 512), BF),
            pltpu.VMEM((256, 512), BF),
            pltpu.VMEM((512, 256), BF),
            pltpu.VMEM((512, 256), F32),
            pltpu.VMEM((2, 2, 512, 128), F32),
            pltpu.VMEM((2, 2, EXT, TILE), BF),
            pltpu.VMEM((2, 2, EXT, TILE), BF),
            pltpu.VMEM((2, 2, TILE, TILE), BF),
            pltpu.VMEM((2, 2, TILE, TILE), BF),
            pltpu.VMEM((2, TILE, TILE), BF),
            pltpu.VMEM((8, 2, STRIP, TILE), BF),
            pltpu.VMEM((8, 2, STRIP, TILE), BF),
            pltpu.VMEM((8, 2, STRIP, TILE), BF),
            pltpu.VMEM((256, 384), F32),
            pltpu.VMEM((PAIRS, 256, 384), BF),
            pltpu.VMEM((4, 256, 768), BF),
            pltpu.VMEM((16, 768), F32),
            pltpu.VMEM((16, 768), BF),
            pltpu.VMEM((128, 512), BF),
            pltpu.VMEM((512, 512), BF),
            pltpu.VMEM((4, 128, 512), BF),
            pltpu.VMEM((2, 272, 128), F32),
            pltpu.VMEM((256, 384), BF),
            pltpu.VMEM((PAIRS, 256, 256), BF),
            pltpu.VMEM((PAIRS, 256, 256), BF),
            pltpu.VMEM((PAIRS, 256, 128), BF),
            pltpu.VMEM((PAIRS, 256, 128), BF),
            pltpu.VMEM((2, 272, 128), F32),
            pltpu.VMEM((4, 32, 256), F32),
            dma((3,)),
            dma((6,)),
            dma((6,)),
            dma((4,)),
            dma((4,)),
            dma((7,)),
            dma((7,)),
            dma((7,)),
            dma((7,)),
        ],
        compiler_params=pltpu.CompilerParams(
            collective_id=0, has_side_effects=True, vmem_limit_bytes=48 * 1024 * 1024
        ),
    )(
        offsets,
        probe_field,
        amplitudes.reshape(POSITIONS, PROBE, PROBE),
        data_state,
        prior_state,
        first_weights,
        middle_weights,
        last_weights,
        table,
    )


def solution(mesh):
    tiles = P(None, ("agent", "row"), "col")
    strips = P(None, ("agent", "row", "col"), None)
    in_specs = (P(), tiles, P(("agent", "row"), "col", None, None), tiles, strips, P(), P(), P())
    return jax.shard_map(
        on_device, mesh=mesh, in_specs=in_specs, out_specs=(tiles, strips), check_vma=False
    )
```

```python
import functools
import math

import jax
import jax.numpy as jnp
import numpy as np
from jax import lax
from jax.experimental import pallas as pl
from jax.experimental.pallas import tpu as pltpu
from jax.sharding import PartitionSpec as P

PROBE = 256
STEP = 64
JITTER = 32
TILE = 128
STRIP = 16
LAYERS = 6
EXT = 384
QUADS = 256
PAIRS = 13
POSITIONS = 4

BF = jnp.bfloat16
F32 = jnp.float32
MESH = pl.DeviceIdType.MESH


def fourier_table():
    numbers = np.arange(PROBE)
    product = (numbers[:, None] * numbers[None, :]) % PROBE
    angles = product * (2.0 * math.pi / PROBE)
    scaling = 1.0 / math.sqrt(PROBE)
    return np.stack([np.cos(angles) * scaling, -np.sin(angles) * scaling]).astype(np.float32)


def dot(left, right):
    return lax.dot_general(left, right, (((1,), (0,)), ((), ())), preferred_element_type=F32)


def dot_nt(left, right):
    return lax.dot_general(left, right, (((1,), (1,)), ((), ())), preferred_element_type=F32)


def slot_of(row, column):
    return column ^ 1 if row else column


def center_lane(row, column):
    return (row // 2) * 256 + (row % 2) * 128 + slot_of(row % 2, column) * 32


def edge_lane(row, column):
    odd = row % 2
    slot = (1 if odd else 0) if column == 4 else (2 if odd else 3)
    return 512 + (row // 2) * 128 + slot * 32


def input_lane(row, column):
    return center_lane(row, column) if 0 <= column < 4 else edge_lane(row, column)


def kernel(
    offsets,
    probe_any,
    amps_any,
    ds_any,
    ps_any,
    first_ref,
    middle_any,
    last_ref,
    table_any,
    data_any,
    prior_any,
    ds_ref,
    middle_ref,
    table_ref,
    data_out,
    prior_out,
    probe,
    amps,
    xf,
    obh,
    obl,
    obr,
    gsend,
    grecv,
    rsend,
    rrecv,
    drb,
    drs,
    prb,
    prt,
    obj,
    acc,
    ff,
    gg,
    ex,
    hs,
    wave,
    cp,
    t1,
    tm,
    t6,
    t6b,
    d2,
    p2,
    xr,
    xv,
    a0,
    a1,
    e0,
    e1,
    zz,
    osc,
    local_sem,
    halo_send,
    halo_recv,
    grad_send,
    grad_recv,
    dr_send,
    dr_recv,
    pr_send,
    pr_recv,
):
    agent, row, col = lax.axis_index("agent"), lax.axis_index("row"), lax.axis_index("col")
    tile_row = agent * 8 + row
    strip = tile_row * 8 + col

    def at(tile, column):
        return (lax.div(tile, 8), lax.rem(tile, 8), column)

    up = at(lax.rem(tile_row + 15, 16), col)
    down = at(lax.rem(tile_row + 1, 16), col)
    left = (agent, row, lax.rem(col + 7, 8))
    right = (agent, row, lax.rem(col + 1, 8))
    before, after = lax.rem(strip + 127, 128), lax.rem(strip + 1, 128)
    prev_strip = at(lax.div(before, 8), lax.rem(before, 8))
    next_strip = at(lax.div(after, 8), lax.rem(after, 8))
    peers = [lax.rem(col + k, 8) for k in range(1, 8)]

    def remote(src, dst, send, recv, device):
        return pltpu.make_async_remote_copy(
            src_ref=src, dst_ref=dst, send_sem=send, recv_sem=recv, device_id=device, device_id_type=MESH
        )

    loads = [
        pltpu.make_async_copy(source, target, local_sem.at[k])
        for k, (source, target) in enumerate(
            (
                (ds_any, ds_ref),
                (ps_any, xf.at[:, 8:24, :]),
                (middle_any, middle_ref),
                (table_any, table_ref),
                (probe_any, probe),
                (amps_any, amps),
            )
        )
    ]
    for load in loads:
        load.start()

    barrier = pltpu.get_barrier_semaphore()
    greeted = [up, down, prev_strip, next_strip] + [(agent, row, c) for c in peers]
    for device in greeted:
        pl.semaphore_signal(barrier, inc=1, device_id=device, device_id_type=MESH)
    loads[0].wait()
    loads[1].wait()
    obh[:, 128:256, :] = ds_ref[...].astype(BF)
    pl.semaphore_wait(barrier, len(greeted))

    to_prev = remote(xf.at[:, 8:16, :], xf.at[:, 24:32, :], halo_send.at[0], halo_recv.at[0], prev_strip)
    to_next = remote(xf.at[:, 16:24, :], xf.at[:, 0:8, :], halo_send.at[1], halo_recv.at[1], next_strip)
    to_down = remote(obh.at[:, 128:256, :], obh.at[:, 0:128, :], halo_send.at[2], halo_recv.at[2], down)
    to_up = remote(obh.at[:, 128:256, :], obh.at[:, 256:384, :], halo_send.at[3], halo_recv.at[3], up)
    for copy in (to_prev, to_next, to_down, to_up):
        copy.start()

    for load in loads[2:4]:
        load.wait()
    t6[...] = jnp.zeros_like(t6)
    for r in range(2):
        for c in range(4):
            for a in range(3):
                for b in range(3):
                    lane = input_lane(r + a, c + b - 1)
                    t6[r * 8 + c * 2 : r * 8 + c * 2 + 2, lane : lane + 32] = last_ref[
                        a, :, 32 * b : 32 * b + 32
                    ].astype(F32)
    t6b[...] = t6[...].astype(BF)

    def banded(value_of, r, line, place, height):
        slots = lax.broadcasted_iota(jnp.int32, (height, 128), 1) // 32
        total = jnp.zeros((height, 128), F32)
        if 0 <= line - r <= 2:
            for b in range(3):
                c = place - b + 1
                if 0 <= c < 4:
                    total = jnp.where(slots == slot_of(r, c), value_of(line - r, b), total)
        return total

    for layer in range(4):
        turned = []
        for a in range(3):
            block = jnp.transpose(middle_ref[layer, a].astype(F32))
            turned.append(jnp.concatenate([block] * 4, axis=1))
        for line in range(4):
            for place in range(-1, 5):
                lane = input_lane(line, place)
                for r in range(2):
                    tm[layer, lane : lane + 32, 128 * r : 128 * r + 128] = banded(
                        lambda a, b: turned[a][32 * b : 32 * b + 32], r, line, place, 32
                    ).astype(BF)

    t1[...] = jnp.zeros_like(t1)
    firsts = [jnp.concatenate([first_ref[a].astype(F32)] * 4, axis=1) for a in range(3)]
    for line in range(4):
        for place in range(-1, 5):
            if 0 <= place < 4:
                lane = (place % 2) * 64 + 4 * (place // 2) + line
            else:
                lane = (0 if place == 4 else 64) + 8 + line
            for k in range(2):
                for r in range(2):
                    t1[lane + 32 * k : lane + 32 * k + 1, 128 * r : 128 * r + 128] = banded(
                        lambda a, b: firsts[a][2 * b + k : 2 * b + k + 1], r, line, place, 1
                    )

    vq = lax.broadcasted_iota(jnp.int32, (128, 512), 0)
    jc = lax.broadcasted_iota(jnp.int32, (128, 512), 1)
    hit = lax.rem(jc, 256) == 4 * lax.rem(vq, 64) + 2 * lax.div(vq, 64) + lax.div(jc, 256)
    d2[...] = jnp.where(hit, 1.0, 0.0).astype(BF)
    jq = lax.broadcasted_iota(jnp.int32, (512, 512), 0)
    cc = lax.broadcasted_iota(jnp.int32, (512, 512), 1)
    p2[...] = jnp.where(cc == 4 * lax.rem(jq, 128) + lax.div(jq, 128), 1.0, 0.0).astype(BF)

    real, imag = table_ref[0], table_ref[1]
    minus = (-imag.astype(F32)).astype(BF)
    ff[0:256, 0:256] = real
    ff[0:256, 256:512] = imag
    ff[256:512, 0:256] = minus
    ff[256:512, 256:512] = real
    gg[0:256, 0:256] = real
    gg[0:256, 256:512] = minus
    gg[256:512, 0:256] = imag
    gg[256:512, 256:512] = real

    to_prev.wait()
    to_next.wait()
    xr[...] = jnp.zeros_like(xr)
    zero_rows = jnp.zeros((8, 128), F32)
    for slot in range(2):
        xv[slot, 0:8, :] = zero_rows
        xv[slot, 264:272, :] = zero_rows
    for slot in range(4):
        zz[slot, 0:8, :] = zero_rows
        zz[slot, 264:272, :] = zero_rows
    keep_top = strip > 0
    keep_bottom = strip < 127
    for t in range(4):
        cols = slice(256 * t, 256 * t + 256)
        for k in range(2):
            piece = jnp.concatenate(
                [
                    jnp.where(keep_top, xf[k, 0:8, cols], 0.0),
                    xf[k, 8:24, cols],
                    jnp.where(keep_bottom, xf[k, 24:32, cols], 0.0),
                ],
                axis=0,
            ).astype(BF)
            xr[t, 32 * k : 32 * k + 32, 0:256] = piece
            xr[t, 64 + 32 * k : 96 + 32 * k, 256:512] = piece
        spread = dot_nt(d2[...], xr[t])
        xv[0, 8 + 64 * t : 72 + 64 * t, :] = spread[0:64]
        xv[1, 8 + 64 * t : 72 + 64 * t, :] = spread[64:128]
    wide_ids = lax.broadcasted_iota(jnp.int32, (QUADS, 128), 1)
    low_half = wide_ids < 64
    outer = (wide_ids < 32) | (wide_ids >= 96)

    to_down.wait()
    to_up.wait()
    to_right = remote(obh, obl, halo_send.at[4], halo_recv.at[4], right)
    to_left = remote(obh, obr, halo_send.at[5], halo_recv.at[5], left)
    to_right.start()
    to_left.start()

    def finish(y, first, pair, slot, a_out, e_out):
        top = first + 2 * pair
        in_top = (top >= 0) & (top < 2048)
        in_low = (top >= -1) & (top < 2047)
        y0 = jnp.where(in_top, jnp.maximum(y[:, 0:128], 0.0), 0.0)
        y1 = jnp.where(in_low, jnp.maximum(y[:, 128:256], 0.0), 0.0)
        a_out[pair, :, 0:128] = y0.astype(BF)
        a_out[pair, :, 128:256] = y1.astype(BF)
        zz[slot, 8:264, :] = jnp.where(outer, y0, y1)
        e_out[pair] = jnp.where(low_half, zz[slot, 9:265, :], zz[slot, 7:263, :]).astype(BF)

    base = strip * STRIP - LAYERS
    within = wide_ids & 31
    edges = jnp.where(low_half, xv[0, 9:265, :], xv[1, 7:263, :])

    def groups(count):
        parts = -(-count // 4)
        bounds = [count * k // parts for k in range(parts + 1)]
        return list(zip(bounds[:-1], bounds[1:]))

    for low, high in groups(PAIRS):
        taken = []
        for pair in range(low, high):
            shift = 128 - 2 - 2 * pair
            near = pltpu.roll(xv[0, 8:264, :], shift, 1)
            far = pltpu.roll(xv[1, 8:264, :], (shift + 4) % 128, 1)
            rest = pltpu.roll(edges, (shift + 8) % 128, 1)
            taken.append(jnp.where(within < 4, near, jnp.where(within < 8, far, rest)).astype(BF))
        y = dot(jnp.concatenate(taken, axis=0), t1[...].astype(BF))
        for pair in range(low, high):
            k = pair - low
            finish(y[256 * k : 256 * k + 256], base + 1, pair, k, a0, e0)

    def window(a_in, e_in, low, high):
        rows = (high - low) * QUADS
        parts = [
            a_in[low:high].reshape(rows, 256),
            a_in[low + 1 : high + 1].reshape(rows, 256),
            e_in[low:high].reshape(rows, 128),
            e_in[low + 1 : high + 1].reshape(rows, 128),
        ]
        return jnp.concatenate(parts, axis=1)

    def middle_layer(depth, a_in, e_in, a_out, e_out):
        for low, high in groups(PAIRS + 1 - depth):
            y = dot(window(a_in, e_in, low, high), tm[depth - 2])
            for pair in range(low, high):
                k = pair - low
                finish(y[256 * k : 256 * k + 256], base + depth, pair, k, a_out, e_out)

    middle_layer(2, a0, e0, a1, e1)

    to_right.wait()
    to_left.wait()
    loads[4].wait()
    loads[5].wait()
    for part in range(2):
        for block, source in enumerate((obl, obh, obr)):
            column_in = (col > 0, True, col < 7)[block]
            for third in range(3):
                rows = slice(128 * third, 128 * third + 128)
                if block == 1 and third == 1:
                    value = ds_ref[part]
                else:
                    inside = (tile_row > 0, True, tile_row < 15)[third]
                    keep = jnp.logical_and(inside, column_in)
                    value = jnp.where(keep, source[part, rows, :].astype(F32), 0.0)
                obj[part, block, rows, :] = value
    for part in range(2):
        for number in range(POSITIONS):
            for block in range(2):
                cp[number, part, block, 0:128, :] = jnp.zeros((128, 128), F32)
                cp[number, part, block, 384:512, :] = jnp.zeros((128, 128), F32)

    places = []
    for number in range(POSITIONS):
        grid_row, grid_col = divmod(number, 2)
        places.append(
            (
                grid_row * STEP + JITTER + offsets[0, grid_row, grid_col],
                grid_col * STEP + JITTER + offsets[1, grid_row, grid_col],
            )
        )

    def transform(first, second):
        for number in range(0, POSITIONS, 2):
            rows = slice(256 * number, 256 * number + 512)
            for part in range(2):
                half = dot(ex[rows, :], first[:, 256 * part : 256 * part + 256]).astype(BF)
                for k in range(2):
                    hs[number + k, 256 * part : 256 * part + 256, :] = half[256 * k : 256 * k + 256]
        for number in range(POSITIONS):
            wave[number] = dot(second[...], hs[number])

    for number, (upper, lefty) in enumerate(places):
        back_roll = lax.rem(EXT - lefty, EXT)
        for chunk in range(0, PROBE, 64):
            rows = slice(chunk, chunk + 64)
            o_r, o_i = [
                pltpu.roll(
                    jnp.concatenate(
                        [obj[part, block, pl.ds(upper + chunk, 64), :] for block in range(3)], axis=1
                    ),
                    back_roll,
                    1,
                )[:, 0:256]
                for part in range(2)
            ]
            p_r, p_i = probe[0, rows, :], probe[1, rows, :]
            out = slice(256 * number + chunk, 256 * number + chunk + 64)
            ex[out, 0:256] = (p_r * o_r - p_i * o_i).astype(BF)
            ex[out, 256:512] = (p_r * o_i + p_i * o_r).astype(BF)
    transform(ff, gg)
    for number in range(POSITIONS):
        for chunk in range(0, PROBE, 64):
            rows = slice(chunk, chunk + 64)
            w_r, w_i = wave[number, rows, :], wave[number, 256 + chunk : 320 + chunk, :]
            square = w_r * w_r + w_i * w_i
            retained = 1.0 - amps[number, rows, :] * lax.rsqrt(jnp.maximum(square, 0.25))
            out = slice(256 * number + chunk, 256 * number + chunk + 64)
            ex[out, 0:256] = (w_r * retained).astype(BF)
            ex[out, 256:512] = (w_i * retained).astype(BF)
    transform(gg, ff)
    for number, (upper, lefty) in enumerate(places):
        for chunk in range(0, PROBE, 64):
            rows = slice(chunk, chunk + 64)
            f_r, f_i = wave[number, rows, :], wave[number, 256 + chunk : 320 + chunk, :]
            p_r, p_i = probe[0, rows, :], probe[1, rows, :]
            for part, term in enumerate((p_r * f_r + p_i * f_i, p_r * f_i - p_i * f_r)):
                for block in range(2):
                    cp[number, part, block, 128 + chunk : 192 + chunk, :] = term[
                        :, 128 * block : 128 * block + 128
                    ]
    for part in range(2):
        for chunk in range(0, EXT, 64):
            total = None
            for number, (upper, lefty) in enumerate(places):
                term = [cp[number, part, block, pl.ds(128 - upper + chunk, 64), :] for block in range(2)]
                term = jnp.concatenate(term + [jnp.zeros((64, 128), F32)], axis=1)
                term = pltpu.roll(term, lefty, 1)
                total = term if total is None else total + term
            acc[part, chunk : chunk + 64, :] = total

    for part in range(2):
        gsend[0, part] = acc[part, :, 0:128].astype(BF)
        gsend[1, part] = acc[part, :, 256:384].astype(BF)
    grad_left = remote(gsend.at[0], grecv.at[1], grad_send.at[0], grad_recv.at[0], left)
    grad_right = remote(gsend.at[1], grecv.at[0], grad_send.at[1], grad_recv.at[1], right)
    grad_left.start()
    grad_right.start()

    middle_layer(3, a1, e1, a0, e0)

    grad_left.wait()
    grad_right.wait()
    keeps = (col > 0, col < 7)
    for part in range(2):
        total = acc[part, :, 128:256]
        for side in range(2):
            total = total + jnp.where(keeps[side], grecv[side, part].astype(F32), 0.0)
        acc[part, :, 128:256] = total
        rsend[0, part] = total[0:128].astype(BF)
        rsend[1, part] = total[256:384].astype(BF)
    grad_up = remote(rsend.at[0], rrecv.at[1], grad_send.at[2], grad_recv.at[2], up)
    grad_down = remote(rsend.at[1], rrecv.at[0], grad_send.at[3], grad_recv.at[3], down)
    grad_up.start()
    grad_down.start()

    middle_layer(4, a0, e0, a1, e1)

    grad_up.wait()
    grad_down.wait()
    keeps_row = (tile_row > 0, tile_row < 15)
    for part in range(2):
        total = acc[part, 128:256, 128:256]
        for side in range(2):
            total = total + jnp.where(keeps_row[side], rrecv[side, part].astype(F32), 0.0)
        reflect = ds_ref[part] - 0.25 * total
        acc[part, 128:256, 128:256] = reflect
        drb[part] = reflect.astype(BF)
    dr_copies = []
    for k, c in enumerate(peers):
        dr_copies.append(
            remote(
                drb.at[:, pl.ds(pl.multiple_of(c * STRIP, STRIP), STRIP), :],
                drs.at[col],
                dr_send.at[k],
                dr_recv.at[k],
                (agent, row, c),
            )
        )
        dr_copies[-1].start()
    drs[col] = drb[:, pl.ds(pl.multiple_of(col * STRIP, STRIP), STRIP), :]

    middle_layer(5, a1, e1, a0, e0)

    for pair in range(STRIP // 2):
        y = dot_nt(t6b[...], window(a0, e0, pair, pair + 1))
        for r in range(2):
            for c in range(4):
                for k in range(2):
                    at_row = k * STRIP + 2 * pair + r
                    osc[c, at_row : at_row + 1, :] = y[r * 8 + c * 2 + k : r * 8 + c * 2 + k + 1, :]

    for half in range(2):
        joined = jnp.concatenate([osc[c, :, 128 * half : 128 * half + 128] for c in range(4)], axis=1)
        coarse = joined.astype(BF)
        fine = (joined - coarse.astype(F32)).astype(BF)
        both = dot(jnp.concatenate([coarse, fine], axis=0), p2[...])
        noise = both[0:32] + both[32:64]
        for k in range(2):
            cols = slice(512 * half, 512 * half + 512)
            reflect = xf[k, 8:24, cols] - 2.0 * noise[16 * k : 16 * k + 16]
            prior_out[k, :, cols] = 0.5 * xf[k, 8:24, cols] - 0.1 * reflect
            for c in range(4):
                prb[4 * half + c, k] = reflect[:, 128 * c : 128 * c + 128].astype(BF)
    pr_copies = []
    for k, c in enumerate(peers):
        pr_copies.append(remote(prb.at[c], prt.at[col], pr_send.at[k], pr_recv.at[k], (agent, row, c)))
        pr_copies[-1].start()
    prt[col] = prb[col]

    for copy in dr_copies:
        copy.wait()
    for c in range(8):
        cols = slice(128 * c, 128 * c + 128)
        for k in range(2):
            prior_out[k, :, cols] = prior_out[k, :, cols] + 0.6 * drs[c, k].astype(F32)
    store_prior = pltpu.make_async_copy(prior_out, prior_any, local_sem.at[8])
    store_prior.start()
    for copy in pr_copies:
        copy.wait()
    for c in range(8):
        rows = slice(STRIP * c, STRIP * c + STRIP)
        for k in range(2):
            data_out[k, rows, :] = (
                0.5 * ds_ref[k, rows, :]
                + 0.1 * acc[k, 128 + STRIP * c : 144 + STRIP * c, 128:256]
                + 0.4 * prt[c, k].astype(F32)
            )
    store_data = pltpu.make_async_copy(data_out, data_any, local_sem.at[9])
    store_data.start()
    store_prior.wait()
    store_data.wait()


def on_device(
    probe_field, offsets, amplitudes, data_state, prior_state, first_weights, middle_weights, last_weights
):
    hbm = pl.BlockSpec(memory_space=pltpu.HBM)
    vmem = pl.BlockSpec(memory_space=pltpu.VMEM)
    table = jnp.asarray(fourier_table()).astype(BF)
    dma = pltpu.SemaphoreType.DMA
    return pl.pallas_call(
        kernel,
        name="step",
        out_shape=(
            jax.ShapeDtypeStruct((2, TILE, TILE), F32),
            jax.ShapeDtypeStruct((2, STRIP, 1024), F32),
        ),
        in_specs=[
            pl.BlockSpec(memory_space=pltpu.SMEM),
            hbm,
            hbm,
            hbm,
            hbm,
            vmem,
            hbm,
            vmem,
            hbm,
        ],
        out_specs=(hbm, hbm),
        scratch_shapes=[
            pltpu.VMEM((2, TILE, TILE), F32),
            pltpu.VMEM((4, 3, 32, 96), BF),
            pltpu.VMEM((2, 256, 256), BF),
            pltpu.VMEM((2, TILE, TILE), F32),
            pltpu.VMEM((2, STRIP, 1024), F32),
            pltpu.VMEM((2, PROBE, PROBE), F32),
            pltpu.VMEM((POSITIONS, PROBE, PROBE), F32),
            pltpu.VMEM((2, 32, 1024), F32),
            pltpu.VMEM((2, EXT, TILE), BF),
            pltpu.VMEM((2, EXT, TILE), BF),
            pltpu.VMEM((2, EXT, TILE), BF),
            pltpu.VMEM((2, 2, EXT, TILE), BF),
            pltpu.VMEM((2, 2, EXT, TILE), BF),
            pltpu.VMEM((2, 2, TILE, TILE), BF),
            pltpu.VMEM((2, 2, TILE, TILE), BF),
            pltpu.VMEM((2, TILE, TILE), BF),
            pltpu.VMEM((8, 2, STRIP, TILE), BF),
            pltpu.VMEM((8, 2, STRIP, TILE), BF),
            pltpu.VMEM((8, 2, STRIP, TILE), BF),
            pltpu.VMEM((2, 3, EXT, TILE), F32),
            pltpu.VMEM((2, EXT, EXT), F32),
            pltpu.VMEM((512, 512), BF),
            pltpu.VMEM((512, 512), BF),
            pltpu.VMEM((1024, 512), BF),
            pltpu.VMEM((4, 512, 256), BF),
            pltpu.VMEM((4, 512, 256), F32),
            pltpu.VMEM((4, 2, 2, 512, 128), F32),
            pltpu.VMEM((128, 256), F32),
            pltpu.VMEM((4, 768, 256), BF),
            pltpu.VMEM((16, 768), F32),
            pltpu.VMEM((16, 768), BF),
            pltpu.VMEM((128, 512), BF),
            pltpu.VMEM((512, 512), BF),
            pltpu.VMEM((4, 128, 512), BF),
            pltpu.VMEM((2, 272, 128), F32),
            pltpu.VMEM((PAIRS, 256, 256), BF),
            pltpu.VMEM((PAIRS, 256, 256), BF),
            pltpu.VMEM((PAIRS, 256, 128), BF),
            pltpu.VMEM((PAIRS, 256, 128), BF),
            pltpu.VMEM((4, 272, 128), F32),
            pltpu.VMEM((4, 32, 256), F32),
            dma((10,)),
            dma((6,)),
            dma((6,)),
            dma((4,)),
            dma((4,)),
            dma((7,)),
            dma((7,)),
            dma((7,)),
            dma((7,)),
        ],
        compiler_params=pltpu.CompilerParams(
            collective_id=0, has_side_effects=True, vmem_limit_bytes=61 * 1024 * 1024
        ),
    )(
        offsets,
        probe_field,
        amplitudes.reshape(POSITIONS, PROBE, PROBE),
        data_state,
        prior_state,
        jnp.transpose(first_weights, (0, 2, 1)),
        middle_weights,
        last_weights,
        table,
    )


def solution(mesh):
    tiles = P(None, ("agent", "row"), "col")
    strips = P(None, ("agent", "row", "col"), None)
    in_specs = (P(), tiles, P(("agent", "row"), "col", None, None), tiles, strips, P(), P(), P())
    return jax.shard_map(
        on_device, mesh=mesh, in_specs=in_specs, out_specs=(tiles, strips), check_vma=False
    )
```

```python
import functools
import math

import jax
import jax.numpy as jnp
import numpy as np
from jax import lax
from jax.experimental import pallas as pl
from jax.experimental.pallas import tpu as pltpu
from jax.sharding import PartitionSpec as P

PROBE = 256
STEP = 64
JITTER = 32
TILE = 128
STRIP = 16
LAYERS = 6
EXT = 384
QUADS = 256
PAIRS = 13
POSITIONS = 4

BF = jnp.bfloat16
F32 = jnp.float32
MESH = pl.DeviceIdType.MESH


def fourier_table():
    numbers = np.arange(PROBE)
    product = (numbers[:, None] * numbers[None, :]) % PROBE
    angles = product * (2.0 * math.pi / PROBE)
    scaling = 1.0 / math.sqrt(PROBE)
    return np.stack([np.cos(angles) * scaling, -np.sin(angles) * scaling]).astype(np.float32)


def dot(left, right):
    return lax.dot_general(left, right, (((1,), (0,)), ((), ())), preferred_element_type=F32)


def dot_nt(left, right):
    return lax.dot_general(left, right, (((1,), (1,)), ((), ())), preferred_element_type=F32)


def slot_of(row, column):
    return column ^ 1 if row else column


def center_lane(row, column):
    return (row // 2) * 256 + (row % 2) * 128 + slot_of(row % 2, column) * 32


def edge_lane(row, column):
    odd = row % 2
    slot = (1 if odd else 0) if column == 4 else (2 if odd else 3)
    return 512 + (row // 2) * 128 + slot * 32


def input_lane(row, column):
    return center_lane(row, column) if 0 <= column < 4 else edge_lane(row, column)


def kernel(
    offsets,
    probe_any,
    amps_any,
    ds_any,
    ps_any,
    first_ref,
    middle_any,
    last_ref,
    table_any,
    data_any,
    prior_any,
    ds_ref,
    middle_ref,
    table_ref,
    data_out,
    prior_out,
    probe,
    amps,
    xf,
    hsend,
    hrecv,
    obh,
    obl,
    obr,
    gsend,
    grecv,
    rsend,
    rrecv,
    drb,
    drs,
    prb,
    prt,
    obj,
    acc,
    ff,
    gg,
    ex,
    hs,
    wave,
    cp,
    t1,
    tm,
    t6,
    t6b,
    d2,
    p2,
    xr,
    xv,
    a0,
    a1,
    e0,
    e1,
    zz,
    osc,
    local_sem,
    halo_send,
    halo_recv,
    grad_send,
    grad_recv,
    dr_send,
    dr_recv,
    pr_send,
    pr_recv,
):
    agent, row, col = lax.axis_index("agent"), lax.axis_index("row"), lax.axis_index("col")
    tile_row = agent * 8 + row
    strip = tile_row * 8 + col

    def at(tile, column):
        return (lax.div(tile, 8), lax.rem(tile, 8), column)

    up = at(lax.rem(tile_row + 15, 16), col)
    down = at(lax.rem(tile_row + 1, 16), col)
    left = (agent, row, lax.rem(col + 7, 8))
    right = (agent, row, lax.rem(col + 1, 8))
    before, after = lax.rem(strip + 127, 128), lax.rem(strip + 1, 128)
    prev_strip = at(lax.div(before, 8), lax.rem(before, 8))
    next_strip = at(lax.div(after, 8), lax.rem(after, 8))
    peers = [lax.rem(col + k, 8) for k in range(1, 8)]

    def remote(src, dst, send, recv, device):
        return pltpu.make_async_remote_copy(
            src_ref=src, dst_ref=dst, send_sem=send, recv_sem=recv, device_id=device, device_id_type=MESH
        )

    loads = [
        pltpu.make_async_copy(source, target, local_sem.at[k])
        for k, (source, target) in enumerate(
            (
                (ds_any, ds_ref),
                (ps_any, xf.at[:, 8:24, :]),
                (middle_any, middle_ref),
                (table_any, table_ref),
                (probe_any, probe),
                (amps_any, amps),
            )
        )
    ]
    for load in loads:
        load.start()

    barrier = pltpu.get_barrier_semaphore()
    greeted = [up, down, prev_strip, next_strip] + [(agent, row, c) for c in peers]
    for device in greeted:
        pl.semaphore_signal(barrier, inc=1, device_id=device, device_id_type=MESH)
    loads[0].wait()
    loads[1].wait()
    obh[:, 128:256, :] = ds_ref[...].astype(BF)
    for side in range(2):
        rows = slice(8 + 8 * side, 16 + 8 * side)
        hsend[side] = jnp.concatenate([xf[0, rows, :], xf[1, rows, :]], axis=0).astype(BF)
    pl.semaphore_wait(barrier, len(greeted))

    def started(copies):
        for copy in copies:
            copy.start()
        return copies

    def finished(copies):
        for copy in copies:
            copy.wait()

    def halo(src, dst, number, device):
        return remote(src, dst, halo_send.at[number], halo_recv.at[number], device)

    def grad(src, dst, number, device):
        return remote(src, dst, grad_send.at[number], grad_recv.at[number], device)

    thirds = [slice(128 * k, 128 * k + 128) for k in range(3)]
    strip_halo = started(
        [
            halo(hsend.at[0], hrecv.at[1], 0, prev_strip),
            halo(hsend.at[1], hrecv.at[0], 1, next_strip),
        ]
    )
    row_halo = []
    for part in range(2):
        own = obh.at[part, thirds[1], :]
        row_halo.append(
            started(
                [
                    halo(own, obh.at[part, thirds[0], :], 2 + 2 * part, down),
                    halo(own, obh.at[part, thirds[2], :], 3 + 2 * part, up),
                ]
            )
        )
    col_halo = started(
        [
            halo(obh.at[:, thirds[1], :], obl.at[:, thirds[1], :], 6, right),
            halo(obh.at[:, thirds[1], :], obr.at[:, thirds[1], :], 7, left),
        ]
    )

    for load in loads[2:4]:
        load.wait()
    t6[...] = jnp.zeros_like(t6)
    for r in range(2):
        for c in range(4):
            for a in range(3):
                for b in range(3):
                    lane = input_lane(r + a, c + b - 1)
                    t6[r * 8 + c * 2 : r * 8 + c * 2 + 2, lane : lane + 32] = last_ref[
                        a, :, 32 * b : 32 * b + 32
                    ].astype(F32)
    t6b[...] = t6[...].astype(BF)

    def banded(value_of, r, line, place, height):
        slots = lax.broadcasted_iota(jnp.int32, (height, 128), 1) // 32
        total = jnp.zeros((height, 128), F32)
        if 0 <= line - r <= 2:
            for b in range(3):
                c = place - b + 1
                if 0 <= c < 4:
                    total = jnp.where(slots == slot_of(r, c), value_of(line - r, b), total)
        return total

    for layer in range(4):
        turned = []
        for a in range(3):
            block = jnp.transpose(middle_ref[layer, a].astype(F32))
            turned.append(jnp.concatenate([block] * 4, axis=1))
        for line in range(4):
            for place in range(-1, 5):
                lane = input_lane(line, place)
                for r in range(2):
                    tm[layer, lane : lane + 32, 128 * r : 128 * r + 128] = banded(
                        lambda a, b: turned[a][32 * b : 32 * b + 32], r, line, place, 32
                    ).astype(BF)

    t1[...] = jnp.zeros_like(t1)
    firsts = [jnp.concatenate([first_ref[a].astype(F32)] * 4, axis=1) for a in range(3)]
    for line in range(4):
        for place in range(-1, 5):
            if 0 <= place < 4:
                lane = (place % 2) * 64 + 4 * (place // 2) + line
            else:
                lane = (0 if place == 4 else 64) + 8 + line
            for k in range(2):
                for r in range(2):
                    t1[lane + 32 * k : lane + 32 * k + 1, 128 * r : 128 * r + 128] = banded(
                        lambda a, b: firsts[a][2 * b + k : 2 * b + k + 1], r, line, place, 1
                    )

    vq = lax.broadcasted_iota(jnp.int32, (128, 512), 0)
    jc = lax.broadcasted_iota(jnp.int32, (128, 512), 1)
    hit = lax.rem(jc, 256) == 4 * lax.rem(vq, 64) + 2 * lax.div(vq, 64) + lax.div(jc, 256)
    d2[...] = jnp.where(hit, 1.0, 0.0).astype(BF)
    jq = lax.broadcasted_iota(jnp.int32, (512, 512), 0)
    cc = lax.broadcasted_iota(jnp.int32, (512, 512), 1)
    p2[...] = jnp.where(cc == 4 * lax.rem(jq, 128) + lax.div(jq, 128), 1.0, 0.0).astype(BF)

    real, imag = table_ref[0], table_ref[1]
    minus = (-imag.astype(F32)).astype(BF)
    ff[0:256, 0:256] = real
    ff[0:256, 256:512] = imag
    ff[256:512, 0:256] = minus
    ff[256:512, 256:512] = real
    gg[0:256, 0:256] = real
    gg[0:256, 256:512] = minus
    gg[256:512, 0:256] = imag
    gg[256:512, 256:512] = real

    finished(strip_halo)
    xr[...] = jnp.zeros_like(xr)
    zero_rows = jnp.zeros((8, 128), F32)
    for slot in range(2):
        xv[slot, 0:8, :] = zero_rows
        xv[slot, 264:272, :] = zero_rows
    for slot in range(4):
        zz[slot, 0:8, :] = zero_rows
        zz[slot, 264:272, :] = zero_rows
    keep_top = strip > 0
    keep_bottom = strip < 127
    for t in range(4):
        cols = slice(256 * t, 256 * t + 256)
        for k in range(2):
            piece = jnp.concatenate(
                [
                    jnp.where(keep_top, hrecv[0, 8 * k : 8 * k + 8, cols].astype(F32), 0.0),
                    xf[k, 8:24, cols],
                    jnp.where(keep_bottom, hrecv[1, 8 * k : 8 * k + 8, cols].astype(F32), 0.0),
                ],
                axis=0,
            ).astype(BF)
            xr[t, 32 * k : 32 * k + 32, 0:256] = piece
            xr[t, 64 + 32 * k : 96 + 32 * k, 256:512] = piece
        spread = dot_nt(d2[...], xr[t])
        xv[0, 8 + 64 * t : 72 + 64 * t, :] = spread[0:64]
        xv[1, 8 + 64 * t : 72 + 64 * t, :] = spread[64:128]
    wide_ids = lax.broadcasted_iota(jnp.int32, (QUADS, 128), 1)
    low_half = wide_ids < 64
    outer = (wide_ids < 32) | (wide_ids >= 96)

    for part in range(2):
        finished(row_halo[part])
        for k in (0, 2):
            rows = obh.at[part, thirds[k], :]
            number = 8 + 4 * part + 2 * (k // 2)
            col_halo += started(
                [
                    halo(rows, obl.at[part, thirds[k], :], number, right),
                    halo(rows, obr.at[part, thirds[k], :], number + 1, left),
                ]
            )

    def finish(y, first, pair, slot, a_out, e_out):
        top = first + 2 * pair
        in_top = (top >= 0) & (top < 2048)
        in_low = (top >= -1) & (top < 2047)
        y0 = jnp.where(in_top, jnp.maximum(y[:, 0:128], 0.0), 0.0)
        y1 = jnp.where(in_low, jnp.maximum(y[:, 128:256], 0.0), 0.0)
        a_out[pair, :, 0:128] = y0.astype(BF)
        a_out[pair, :, 128:256] = y1.astype(BF)
        zz[slot, 8:264, :] = jnp.where(outer, y0, y1)
        e_out[pair] = jnp.where(low_half, zz[slot, 9:265, :], zz[slot, 7:263, :]).astype(BF)

    base = strip * STRIP - LAYERS
    within = wide_ids & 31
    edges = jnp.where(low_half, xv[0, 9:265, :], xv[1, 7:263, :])

    def groups(count):
        parts = -(-count // 4)
        bounds = [count * k // parts for k in range(parts + 1)]
        return list(zip(bounds[:-1], bounds[1:]))

    for low, high in groups(PAIRS):
        taken = []
        for pair in range(low, high):
            shift = 128 - 2 - 2 * pair
            near = pltpu.roll(xv[0, 8:264, :], shift, 1)
            far = pltpu.roll(xv[1, 8:264, :], (shift + 4) % 128, 1)
            rest = pltpu.roll(edges, (shift + 8) % 128, 1)
            taken.append(jnp.where(within < 4, near, jnp.where(within < 8, far, rest)).astype(BF))
        y = dot(jnp.concatenate(taken, axis=0), t1[...].astype(BF))
        for pair in range(low, high):
            k = pair - low
            finish(y[256 * k : 256 * k + 256], base + 1, pair, k, a0, e0)

    def window(a_in, e_in, low, high):
        rows = (high - low) * QUADS
        parts = [
            a_in[low:high].reshape(rows, 256),
            a_in[low + 1 : high + 1].reshape(rows, 256),
            e_in[low:high].reshape(rows, 128),
            e_in[low + 1 : high + 1].reshape(rows, 128),
        ]
        return jnp.concatenate(parts, axis=1)

    def middle_layer(depth, a_in, e_in, a_out, e_out):
        for low, high in groups(PAIRS + 1 - depth):
            y = dot(window(a_in, e_in, low, high), tm[depth - 2])
            for pair in range(low, high):
                k = pair - low
                finish(y[256 * k : 256 * k + 256], base + depth, pair, k, a_out, e_out)

    middle_layer(2, a0, e0, a1, e1)

    finished(col_halo)
    loads[4].wait()
    loads[5].wait()
    for part in range(2):
        for block, source in enumerate((obl, obh, obr)):
            column_in = (col > 0, True, col < 7)[block]
            for third in range(3):
                rows = slice(128 * third, 128 * third + 128)
                if block == 1 and third == 1:
                    value = ds_ref[part]
                else:
                    inside = (tile_row > 0, True, tile_row < 15)[third]
                    keep = jnp.logical_and(inside, column_in)
                    value = jnp.where(keep, source[part, rows, :].astype(F32), 0.0)
                obj[part, block, rows, :] = value
    for part in range(2):
        for number in range(POSITIONS):
            for block in range(2):
                cp[number, part, block, 0:128, :] = jnp.zeros((128, 128), F32)
                cp[number, part, block, 384:512, :] = jnp.zeros((128, 128), F32)

    places = []
    for number in range(POSITIONS):
        grid_row, grid_col = divmod(number, 2)
        places.append(
            (
                grid_row * STEP + JITTER + offsets[0, grid_row, grid_col],
                grid_col * STEP + JITTER + offsets[1, grid_row, grid_col],
            )
        )

    def transform(first, second):
        for number in range(0, POSITIONS, 2):
            rows = slice(256 * number, 256 * number + 512)
            for part in range(2):
                half = dot(ex[rows, :], first[:, 256 * part : 256 * part + 256]).astype(BF)
                for k in range(2):
                    hs[number + k, 256 * part : 256 * part + 256, :] = half[256 * k : 256 * k + 256]
        for number in range(POSITIONS):
            wave[number] = dot(second[...], hs[number])

    for number, (upper, lefty) in enumerate(places):
        back_roll = lax.rem(EXT - lefty, EXT)
        for chunk in range(0, PROBE, 64):
            rows = slice(chunk, chunk + 64)
            o_r, o_i = [
                pltpu.roll(
                    jnp.concatenate(
                        [obj[part, block, pl.ds(upper + chunk, 64), :] for block in range(3)], axis=1
                    ),
                    back_roll,
                    1,
                )[:, 0:256]
                for part in range(2)
            ]
            p_r, p_i = probe[0, rows, :], probe[1, rows, :]
            out = slice(256 * number + chunk, 256 * number + chunk + 64)
            ex[out, 0:256] = (p_r * o_r - p_i * o_i).astype(BF)
            ex[out, 256:512] = (p_r * o_i + p_i * o_r).astype(BF)
    transform(ff, gg)
    for number in range(POSITIONS):
        for chunk in range(0, PROBE, 64):
            rows = slice(chunk, chunk + 64)
            w_r, w_i = wave[number, rows, :], wave[number, 256 + chunk : 320 + chunk, :]
            square = w_r * w_r + w_i * w_i
            retained = 1.0 - amps[number, rows, :] * lax.rsqrt(jnp.maximum(square, 0.25))
            out = slice(256 * number + chunk, 256 * number + chunk + 64)
            ex[out, 0:256] = (w_r * retained).astype(BF)
            ex[out, 256:512] = (w_i * retained).astype(BF)
    transform(gg, ff)
    for number, (upper, lefty) in enumerate(places):
        for chunk in range(0, PROBE, 64):
            rows = slice(chunk, chunk + 64)
            f_r, f_i = wave[number, rows, :], wave[number, 256 + chunk : 320 + chunk, :]
            p_r, p_i = probe[0, rows, :], probe[1, rows, :]
            for part, term in enumerate((p_r * f_r + p_i * f_i, p_r * f_i - p_i * f_r)):
                for block in range(2):
                    cp[number, part, block, 128 + chunk : 192 + chunk, :] = term[
                        :, 128 * block : 128 * block + 128
                    ]
    end_copies = []
    for part in range(2):
        for chunk in range(0, EXT, 64):
            total = None
            for number, (upper, lefty) in enumerate(places):
                term = [cp[number, part, block, pl.ds(128 - upper + chunk, 64), :] for block in range(2)]
                term = jnp.concatenate(term + [jnp.zeros((64, 128), F32)], axis=1)
                term = pltpu.roll(term, lefty, 1)
                total = term if total is None else total + term
            acc[part, chunk : chunk + 64, :] = total
        gsend[0, part] = acc[part, :, 0:128].astype(BF)
        gsend[1, part] = acc[part, :, 256:384].astype(BF)
        ends = []
        for k in (0, 2):
            for side in range(2):
                ends.append(
                    grad(
                        gsend.at[side, part, thirds[k], :],
                        grecv.at[1 - side, part, thirds[k], :],
                        4 * part + k + side,
                        right if side else left,
                    )
                )
        end_copies.append(started(ends))
    middle_copies = started(
        [
            grad(gsend.at[side, :, thirds[1], :], grecv.at[1 - side, :, thirds[1], :], 8 + side, device)
            for side, device in enumerate((left, right))
        ]
    )

    middle_layer(3, a1, e1, a0, e0)

    keeps = (col > 0, col < 7)
    keeps_row = (tile_row > 0, tile_row < 15)

    def folded(part, k):
        total = acc[part, thirds[k], 128:256]
        for side in range(2):
            total = total + jnp.where(keeps[side], grecv[side, part, thirds[k], :].astype(F32), 0.0)
        return total

    row_copies = []
    for part in range(2):
        finished(end_copies[part])
        rsend[0, part] = folded(part, 0).astype(BF)
        rsend[1, part] = folded(part, 2).astype(BF)
        row_copies += started(
            [
                grad(rsend.at[0, part], rrecv.at[1, part], 10 + 2 * part, up),
                grad(rsend.at[1, part], rrecv.at[0, part], 11 + 2 * part, down),
            ]
        )

    middle_layer(4, a0, e0, a1, e1)

    middle_layer(5, a1, e1, a0, e0)

    for pair in range(STRIP // 2):
        y = dot_nt(t6b[...], window(a0, e0, pair, pair + 1))
        for r in range(2):
            for c in range(4):
                for k in range(2):
                    at_row = k * STRIP + 2 * pair + r
                    osc[c, at_row : at_row + 1, :] = y[r * 8 + c * 2 + k : r * 8 + c * 2 + k + 1, :]

    for half in range(2):
        joined = jnp.concatenate([osc[c, :, 128 * half : 128 * half + 128] for c in range(4)], axis=1)
        coarse = joined.astype(BF)
        fine = (joined - coarse.astype(F32)).astype(BF)
        both = dot(jnp.concatenate([coarse, fine], axis=0), p2[...])
        noise = both[0:32] + both[32:64]
        for k in range(2):
            cols = slice(512 * half, 512 * half + 512)
            reflect = xf[k, 8:24, cols] - 2.0 * noise[16 * k : 16 * k + 16]
            prior_out[k, :, cols] = 0.5 * xf[k, 8:24, cols] - 0.1 * reflect
            for c in range(4):
                prb[4 * half + c, k] = reflect[:, 128 * c : 128 * c + 128].astype(BF)
    pr_copies = []
    for k, c in enumerate(peers):
        pr_copies.append(remote(prb.at[c], prt.at[col], pr_send.at[k], pr_recv.at[k], (agent, row, c)))
        pr_copies[-1].start()
    prt[col] = prb[col]

    finished(middle_copies)
    for part in range(2):
        finished(row_copies[2 * part : 2 * part + 2])
        total = folded(part, 1)
        for side in range(2):
            total = total + jnp.where(keeps_row[side], rrecv[side, part].astype(F32), 0.0)
        reflect = ds_ref[part] - 0.25 * total
        acc[part, 128:256, 128:256] = reflect
        drb[part] = reflect.astype(BF)
    dr_copies = []
    for k, c in enumerate(peers):
        dr_copies.append(
            remote(
                drb.at[:, pl.ds(pl.multiple_of(c * STRIP, STRIP), STRIP), :],
                drs.at[col],
                dr_send.at[k],
                dr_recv.at[k],
                (agent, row, c),
            )
        )
        dr_copies[-1].start()
    drs[col] = drb[:, pl.ds(pl.multiple_of(col * STRIP, STRIP), STRIP), :]

    for copy in dr_copies:
        copy.wait()
    for c in range(8):
        cols = slice(128 * c, 128 * c + 128)
        for k in range(2):
            prior_out[k, :, cols] = prior_out[k, :, cols] + 0.6 * drs[c, k].astype(F32)
    store_prior = pltpu.make_async_copy(prior_out, prior_any, local_sem.at[8])
    store_prior.start()
    for copy in pr_copies:
        copy.wait()
    for c in range(8):
        rows = slice(STRIP * c, STRIP * c + STRIP)
        for k in range(2):
            data_out[k, rows, :] = (
                0.5 * ds_ref[k, rows, :]
                + 0.1 * acc[k, 128 + STRIP * c : 144 + STRIP * c, 128:256]
                + 0.4 * prt[c, k].astype(F32)
            )
    store_data = pltpu.make_async_copy(data_out, data_any, local_sem.at[9])
    store_data.start()
    store_prior.wait()
    store_data.wait()


def on_device(
    probe_field, offsets, amplitudes, data_state, prior_state, first_weights, middle_weights, last_weights
):
    hbm = pl.BlockSpec(memory_space=pltpu.HBM)
    vmem = pl.BlockSpec(memory_space=pltpu.VMEM)
    table = jnp.asarray(fourier_table()).astype(BF)
    dma = pltpu.SemaphoreType.DMA
    return pl.pallas_call(
        kernel,
        name="step",
        out_shape=(
            jax.ShapeDtypeStruct((2, TILE, TILE), F32),
            jax.ShapeDtypeStruct((2, STRIP, 1024), F32),
        ),
        in_specs=[
            pl.BlockSpec(memory_space=pltpu.SMEM),
            hbm,
            hbm,
            hbm,
            hbm,
            vmem,
            hbm,
            vmem,
            hbm,
        ],
        out_specs=(hbm, hbm),
        scratch_shapes=[
            pltpu.VMEM((2, TILE, TILE), F32),
            pltpu.VMEM((4, 3, 32, 96), BF),
            pltpu.VMEM((2, 256, 256), BF),
            pltpu.VMEM((2, TILE, TILE), F32),
            pltpu.VMEM((2, STRIP, 1024), F32),
            pltpu.VMEM((2, PROBE, PROBE), F32),
            pltpu.VMEM((POSITIONS, PROBE, PROBE), F32),
            pltpu.VMEM((2, 32, 1024), F32),
            pltpu.VMEM((2, 16, 1024), BF),
            pltpu.VMEM((2, 16, 1024), BF),
            pltpu.VMEM((2, EXT, TILE), BF),
            pltpu.VMEM((2, EXT, TILE), BF),
            pltpu.VMEM((2, EXT, TILE), BF),
            pltpu.VMEM((2, 2, EXT, TILE), BF),
            pltpu.VMEM((2, 2, EXT, TILE), BF),
            pltpu.VMEM((2, 2, TILE, TILE), BF),
            pltpu.VMEM((2, 2, TILE, TILE), BF),
            pltpu.VMEM((2, TILE, TILE), BF),
            pltpu.VMEM((8, 2, STRIP, TILE), BF),
            pltpu.VMEM((8, 2, STRIP, TILE), BF),
            pltpu.VMEM((8, 2, STRIP, TILE), BF),
            pltpu.VMEM((2, 3, EXT, TILE), F32),
            pltpu.VMEM((2, EXT, EXT), F32),
            pltpu.VMEM((512, 512), BF),
            pltpu.VMEM((512, 512), BF),
            pltpu.VMEM((1024, 512), BF),
            pltpu.VMEM((4, 512, 256), BF),
            pltpu.VMEM((4, 512, 256), F32),
            pltpu.VMEM((4, 2, 2, 512, 128), F32),
            pltpu.VMEM((128, 256), F32),
            pltpu.VMEM((4, 768, 256), BF),
            pltpu.VMEM((16, 768), F32),
            pltpu.VMEM((16, 768), BF),
            pltpu.VMEM((128, 512), BF),
            pltpu.VMEM((512, 512), BF),
            pltpu.VMEM((4, 128, 512), BF),
            pltpu.VMEM((2, 272, 128), F32),
            pltpu.VMEM((PAIRS, 256, 256), BF),
            pltpu.VMEM((PAIRS, 256, 256), BF),
            pltpu.VMEM((PAIRS, 256, 128), BF),
            pltpu.VMEM((PAIRS, 256, 128), BF),
            pltpu.VMEM((4, 272, 128), F32),
            pltpu.VMEM((4, 32, 256), F32),
            dma((10,)),
            dma((16,)),
            dma((16,)),
            dma((14,)),
            dma((14,)),
            dma((7,)),
            dma((7,)),
            dma((7,)),
            dma((7,)),
        ],
        compiler_params=pltpu.CompilerParams(
            collective_id=0, has_side_effects=True, vmem_limit_bytes=61 * 1024 * 1024
        ),
    )(
        offsets,
        probe_field,
        amplitudes.reshape(POSITIONS, PROBE, PROBE),
        data_state,
        prior_state,
        jnp.transpose(first_weights, (0, 2, 1)),
        middle_weights,
        last_weights,
        table,
    )


def solution(mesh):
    tiles = P(None, ("agent", "row"), "col")
    strips = P(None, ("agent", "row", "col"), None)
    in_specs = (P(), tiles, P(("agent", "row"), "col", None, None), tiles, strips, P(), P(), P())
    return jax.shard_map(
        on_device, mesh=mesh, in_specs=in_specs, out_specs=(tiles, strips), check_vma=False
    )
```

```python
import functools
import math

import jax
import jax.numpy as jnp
import numpy as np
from jax import lax
from jax.experimental import pallas as pl
from jax.experimental.pallas import tpu as pltpu
from jax.sharding import PartitionSpec as P

PROBE = 256
STEP = 64
JITTER = 32
TILE = 128
STRIP = 16
LAYERS = 6
EXT = 384
QUADS = 256
PAIRS = 13
POSITIONS = 4

BF = jnp.bfloat16
F32 = jnp.float32
MESH = pl.DeviceIdType.MESH


def fourier_table():
    numbers = np.arange(PROBE)
    product = (numbers[:, None] * numbers[None, :]) % PROBE
    angles = product * (2.0 * math.pi / PROBE)
    scaling = 1.0 / math.sqrt(PROBE)
    return np.stack([np.cos(angles) * scaling, -np.sin(angles) * scaling]).astype(np.float32)


def dot(left, right):
    return lax.dot_general(left, right, (((1,), (0,)), ((), ())), preferred_element_type=F32)


def dot_nt(left, right):
    return lax.dot_general(left, right, (((1,), (1,)), ((), ())), preferred_element_type=F32)


def slot_of(row, column):
    return column ^ 1 if row else column


def center_lane(row, column):
    return (row // 2) * 256 + (row % 2) * 128 + slot_of(row % 2, column) * 32


def edge_lane(row, column):
    odd = row % 2
    slot = (1 if odd else 0) if column == 4 else (2 if odd else 3)
    return 512 + (row // 2) * 128 + slot * 32


def input_lane(row, column):
    return center_lane(row, column) if 0 <= column < 4 else edge_lane(row, column)


def kernel(
    offsets,
    probe_any,
    amps_any,
    ds_any,
    ps_any,
    first_ref,
    middle_any,
    last_ref,
    table_any,
    data_any,
    prior_any,
    ds_ref,
    middle_ref,
    table_ref,
    data_out,
    prior_out,
    probe,
    amps,
    xf,
    hsend,
    hrecv,
    obh,
    obl,
    obr,
    gsend,
    grecv,
    rsend,
    rrecv,
    drb,
    drs,
    prb,
    prt,
    obj,
    acc,
    ff,
    gg,
    ex,
    hs,
    wave,
    cp,
    t1,
    tm,
    t6,
    t6b,
    d2,
    p2,
    xr,
    xv,
    a0,
    a1,
    e0,
    e1,
    zz,
    osc,
    local_sem,
    halo_send,
    halo_recv,
    grad_send,
    grad_recv,
    dr_send,
    dr_recv,
    pr_send,
    pr_recv,
):
    agent, row, col = lax.axis_index("agent"), lax.axis_index("row"), lax.axis_index("col")
    tile_row = agent * 8 + row
    strip = tile_row * 8 + col

    def at(tile, column):
        return (lax.div(tile, 8), lax.rem(tile, 8), column)

    up = at(lax.rem(tile_row + 15, 16), col)
    down = at(lax.rem(tile_row + 1, 16), col)
    left = (agent, row, lax.rem(col + 7, 8))
    right = (agent, row, lax.rem(col + 1, 8))
    before, after = lax.rem(strip + 127, 128), lax.rem(strip + 1, 128)
    prev_strip = at(lax.div(before, 8), lax.rem(before, 8))
    next_strip = at(lax.div(after, 8), lax.rem(after, 8))
    peers = [lax.rem(col + k, 8) for k in range(1, 8)]

    def remote(src, dst, send, recv, device):
        return pltpu.make_async_remote_copy(
            src_ref=src, dst_ref=dst, send_sem=send, recv_sem=recv, device_id=device, device_id_type=MESH
        )

    loads = [
        pltpu.make_async_copy(source, target, local_sem.at[k])
        for k, (source, target) in enumerate(
            (
                (ds_any, ds_ref),
                (ps_any, xf.at[:, 8:24, :]),
                (middle_any, middle_ref),
                (table_any, table_ref),
                (probe_any, probe),
                (amps_any, amps),
            )
        )
    ]
    for load in loads:
        load.start()

    barrier = pltpu.get_barrier_semaphore()
    greeted = [up, down, prev_strip, next_strip] + [(agent, row, c) for c in peers]
    for device in greeted:
        pl.semaphore_signal(barrier, inc=1, device_id=device, device_id_type=MESH)
    loads[0].wait()
    loads[1].wait()
    obh[:, 128:256, :] = ds_ref[...].astype(BF)
    for side in range(2):
        rows = slice(8 + 8 * side, 16 + 8 * side)
        hsend[side] = jnp.concatenate([xf[0, rows, :], xf[1, rows, :]], axis=0).astype(BF)
    pl.semaphore_wait(barrier, len(greeted))

    def started(copies):
        for copy in copies:
            copy.start()
        return copies

    def finished(copies):
        for copy in copies:
            copy.wait()

    def halo(src, dst, number, device):
        return remote(src, dst, halo_send.at[number], halo_recv.at[number], device)

    def grad(src, dst, number, device):
        return remote(src, dst, grad_send.at[number], grad_recv.at[number], device)

    thirds = [slice(128 * k, 128 * k + 128) for k in range(3)]
    strip_halo = started(
        [
            halo(hsend.at[0], hrecv.at[1], 0, prev_strip),
            halo(hsend.at[1], hrecv.at[0], 1, next_strip),
        ]
    )
    row_halo = []
    for part in range(2):
        own = obh.at[part, thirds[1], :]
        row_halo.append(
            started(
                [
                    halo(own, obh.at[part, thirds[0], :], 2 + 2 * part, down),
                    halo(own, obh.at[part, thirds[2], :], 3 + 2 * part, up),
                ]
            )
        )
    col_halo = started(
        [
            halo(obh.at[:, thirds[1], :], obl.at[:, thirds[1], :], 6, right),
            halo(obh.at[:, thirds[1], :], obr.at[:, thirds[1], :], 7, left),
        ]
    )

    for load in loads[2:4]:
        load.wait()
    t6[...] = jnp.zeros_like(t6)
    for r in range(2):
        for c in range(4):
            for a in range(3):
                for b in range(3):
                    lane = input_lane(r + a, c + b - 1)
                    t6[r * 8 + c * 2 : r * 8 + c * 2 + 2, lane : lane + 32] = last_ref[
                        a, :, 32 * b : 32 * b + 32
                    ].astype(F32)
    t6b[...] = t6[...].astype(BF)

    def banded(value_of, r, line, place, height):
        slots = lax.broadcasted_iota(jnp.int32, (height, 128), 1) // 32
        total = jnp.zeros((height, 128), F32)
        if 0 <= line - r <= 2:
            for b in range(3):
                c = place - b + 1
                if 0 <= c < 4:
                    total = jnp.where(slots == slot_of(r, c), value_of(line - r, b), total)
        return total

    for layer in range(4):
        turned = []
        for a in range(3):
            block = jnp.transpose(middle_ref[layer, a].astype(F32))
            turned.append(jnp.concatenate([block] * 4, axis=1))
        for line in range(4):
            for place in range(-1, 5):
                lane = input_lane(line, place)
                for r in range(2):
                    tm[layer, lane : lane + 32, 128 * r : 128 * r + 128] = banded(
                        lambda a, b: turned[a][32 * b : 32 * b + 32], r, line, place, 32
                    ).astype(BF)

    t1[...] = jnp.zeros_like(t1)
    firsts = [jnp.concatenate([first_ref[a].astype(F32)] * 4, axis=1) for a in range(3)]
    for line in range(4):
        for place in range(-1, 5):
            if 0 <= place < 4:
                lane = (place % 2) * 64 + 4 * (place // 2) + line
            else:
                lane = (0 if place == 4 else 64) + 8 + line
            for k in range(2):
                for r in range(2):
                    t1[lane + 32 * k : lane + 32 * k + 1, 128 * r : 128 * r + 128] = banded(
                        lambda a, b: firsts[a][2 * b + k : 2 * b + k + 1], r, line, place, 1
                    )

    vq = lax.broadcasted_iota(jnp.int32, (128, 512), 0)
    jc = lax.broadcasted_iota(jnp.int32, (128, 512), 1)
    hit = lax.rem(jc, 256) == 4 * lax.rem(vq, 64) + 2 * lax.div(vq, 64) + lax.div(jc, 256)
    d2[...] = jnp.where(hit, 1.0, 0.0).astype(BF)
    jq = lax.broadcasted_iota(jnp.int32, (512, 512), 0)
    cc = lax.broadcasted_iota(jnp.int32, (512, 512), 1)
    p2[...] = jnp.where(cc == 4 * lax.rem(jq, 128) + lax.div(jq, 128), 1.0, 0.0).astype(BF)

    real, imag = table_ref[0], table_ref[1]
    minus = (-imag.astype(F32)).astype(BF)
    ff[0:256, 0:256] = real
    ff[0:256, 256:512] = imag
    ff[256:512, 0:256] = minus
    ff[256:512, 256:512] = real
    gg[0:256, 0:256] = real
    gg[0:256, 256:512] = minus
    gg[256:512, 0:256] = imag
    gg[256:512, 256:512] = real

    for part in range(2):
        finished(row_halo[part])
        for k in (0, 2):
            rows = obh.at[part, thirds[k], :]
            number = 8 + 4 * part + 2 * (k // 2)
            col_halo += started(
                [
                    halo(rows, obl.at[part, thirds[k], :], number, right),
                    halo(rows, obr.at[part, thirds[k], :], number + 1, left),
                ]
            )

    finished(strip_halo)
    xr[...] = jnp.zeros_like(xr)
    zero_rows = jnp.zeros((8, 128), F32)
    for slot in range(2):
        xv[slot, 0:8, :] = zero_rows
        xv[slot, 264:272, :] = zero_rows
    for slot in range(4):
        zz[slot, 0:8, :] = zero_rows
        zz[slot, 264:272, :] = zero_rows
    keep_top = strip > 0
    keep_bottom = strip < 127
    for t in range(4):
        cols = slice(256 * t, 256 * t + 256)
        for k in range(2):
            piece = jnp.concatenate(
                [
                    jnp.where(keep_top, hrecv[0, 8 * k : 8 * k + 8, cols].astype(F32), 0.0),
                    xf[k, 8:24, cols],
                    jnp.where(keep_bottom, hrecv[1, 8 * k : 8 * k + 8, cols].astype(F32), 0.0),
                ],
                axis=0,
            ).astype(BF)
            xr[t, 32 * k : 32 * k + 32, 0:256] = piece
            xr[t, 64 + 32 * k : 96 + 32 * k, 256:512] = piece
        spread = dot_nt(d2[...], xr[t])
        xv[0, 8 + 64 * t : 72 + 64 * t, :] = spread[0:64]
        xv[1, 8 + 64 * t : 72 + 64 * t, :] = spread[64:128]
    wide_ids = lax.broadcasted_iota(jnp.int32, (QUADS, 128), 1)
    low_half = wide_ids < 64
    outer = (wide_ids < 32) | (wide_ids >= 96)

    def finish(y, first, pair, slot, a_out, e_out):
        top = first + 2 * pair
        in_top = (top >= 0) & (top < 2048)
        in_low = (top >= -1) & (top < 2047)
        y0 = jnp.where(in_top, jnp.maximum(y[:, 0:128], 0.0), 0.0)
        y1 = jnp.where(in_low, jnp.maximum(y[:, 128:256], 0.0), 0.0)
        a_out[pair, :, 0:128] = y0.astype(BF)
        a_out[pair, :, 128:256] = y1.astype(BF)
        zz[slot, 8:264, :] = jnp.where(outer, y0, y1)
        e_out[pair] = jnp.where(low_half, zz[slot, 9:265, :], zz[slot, 7:263, :]).astype(BF)

    base = strip * STRIP - LAYERS
    within = wide_ids & 31
    edges = jnp.where(low_half, xv[0, 9:265, :], xv[1, 7:263, :])

    def groups(count):
        parts = -(-count // 4)
        bounds = [count * k // parts for k in range(parts + 1)]
        return list(zip(bounds[:-1], bounds[1:]))

    for low, high in groups(PAIRS):
        taken = []
        for pair in range(low, high):
            shift = 128 - 2 - 2 * pair
            near = pltpu.roll(xv[0, 8:264, :], shift, 1)
            far = pltpu.roll(xv[1, 8:264, :], (shift + 4) % 128, 1)
            rest = pltpu.roll(edges, (shift + 8) % 128, 1)
            taken.append(jnp.where(within < 4, near, jnp.where(within < 8, far, rest)).astype(BF))
        y = dot(jnp.concatenate(taken, axis=0), t1[...].astype(BF))
        for pair in range(low, high):
            k = pair - low
            finish(y[256 * k : 256 * k + 256], base + 1, pair, k, a0, e0)

    def window(a_in, e_in, low, high):
        rows = (high - low) * QUADS
        parts = [
            a_in[low:high].reshape(rows, 256),
            a_in[low + 1 : high + 1].reshape(rows, 256),
            e_in[low:high].reshape(rows, 128),
            e_in[low + 1 : high + 1].reshape(rows, 128),
        ]
        return jnp.concatenate(parts, axis=1)

    def middle_layer(depth, a_in, e_in, a_out, e_out):
        for low, high in groups(PAIRS + 1 - depth):
            y = dot(window(a_in, e_in, low, high), tm[depth - 2])
            for pair in range(low, high):
                k = pair - low
                finish(y[256 * k : 256 * k + 256], base + depth, pair, k, a_out, e_out)

    middle_layer(2, a0, e0, a1, e1)

    finished(col_halo)
    loads[4].wait()
    loads[5].wait()
    for part in range(2):
        for block, source in enumerate((obl, obh, obr)):
            column_in = (col > 0, True, col < 7)[block]
            for third in range(3):
                rows = slice(128 * third, 128 * third + 128)
                if block == 1 and third == 1:
                    value = ds_ref[part]
                else:
                    inside = (tile_row > 0, True, tile_row < 15)[third]
                    keep = jnp.logical_and(inside, column_in)
                    value = jnp.where(keep, source[part, rows, :].astype(F32), 0.0)
                obj[part, block, rows, :] = value
    for part in range(2):
        for number in range(POSITIONS):
            for block in range(2):
                cp[number, part, block, 0:128, :] = jnp.zeros((128, 128), F32)
                cp[number, part, block, 384:512, :] = jnp.zeros((128, 128), F32)

    places = []
    for number in range(POSITIONS):
        grid_row, grid_col = divmod(number, 2)
        places.append(
            (
                grid_row * STEP + JITTER + offsets[0, grid_row, grid_col],
                grid_col * STEP + JITTER + offsets[1, grid_row, grid_col],
            )
        )

    def transform(first, second):
        for number in range(0, POSITIONS, 2):
            rows = slice(256 * number, 256 * number + 512)
            for part in range(2):
                half = dot(ex[rows, :], first[:, 256 * part : 256 * part + 256]).astype(BF)
                for k in range(2):
                    hs[number + k, 256 * part : 256 * part + 256, :] = half[256 * k : 256 * k + 256]
        for number in range(POSITIONS):
            wave[number] = dot(second[...], hs[number])

    for number, (upper, lefty) in enumerate(places):
        back_roll = lax.rem(EXT - lefty, EXT)
        for chunk in range(0, PROBE, 64):
            rows = slice(chunk, chunk + 64)
            o_r, o_i = [
                pltpu.roll(
                    jnp.concatenate(
                        [obj[part, block, pl.ds(upper + chunk, 64), :] for block in range(3)], axis=1
                    ),
                    back_roll,
                    1,
                )[:, 0:256]
                for part in range(2)
            ]
            p_r, p_i = probe[0, rows, :], probe[1, rows, :]
            out = slice(256 * number + chunk, 256 * number + chunk + 64)
            ex[out, 0:256] = (p_r * o_r - p_i * o_i).astype(BF)
            ex[out, 256:512] = (p_r * o_i + p_i * o_r).astype(BF)
    transform(ff, gg)
    for number in range(POSITIONS):
        for chunk in range(0, PROBE, 64):
            rows = slice(chunk, chunk + 64)
            w_r, w_i = wave[number, rows, :], wave[number, 256 + chunk : 320 + chunk, :]
            square = w_r * w_r + w_i * w_i
            retained = 1.0 - amps[number, rows, :] * lax.rsqrt(jnp.maximum(square, 0.25))
            out = slice(256 * number + chunk, 256 * number + chunk + 64)
            ex[out, 0:256] = (w_r * retained).astype(BF)
            ex[out, 256:512] = (w_i * retained).astype(BF)
    transform(gg, ff)
    for number, (upper, lefty) in enumerate(places):
        for chunk in range(0, PROBE, 64):
            rows = slice(chunk, chunk + 64)
            f_r, f_i = wave[number, rows, :], wave[number, 256 + chunk : 320 + chunk, :]
            p_r, p_i = probe[0, rows, :], probe[1, rows, :]
            for part, term in enumerate((p_r * f_r + p_i * f_i, p_r * f_i - p_i * f_r)):
                for block in range(2):
                    cp[number, part, block, 128 + chunk : 192 + chunk, :] = term[
                        :, 128 * block : 128 * block + 128
                    ]
    end_copies = []
    for part in range(2):
        for chunk in range(0, EXT, 64):
            total = None
            for number, (upper, lefty) in enumerate(places):
                term = [cp[number, part, block, pl.ds(128 - upper + chunk, 64), :] for block in range(2)]
                term = jnp.concatenate(term + [jnp.zeros((64, 128), F32)], axis=1)
                term = pltpu.roll(term, lefty, 1)
                total = term if total is None else total + term
            acc[part, chunk : chunk + 64, :] = total
        gsend[0, part] = acc[part, :, 0:128].astype(BF)
        gsend[1, part] = acc[part, :, 256:384].astype(BF)
        ends = []
        for k in (0, 2):
            for side in range(2):
                ends.append(
                    grad(
                        gsend.at[side, part, thirds[k], :],
                        grecv.at[1 - side, part, thirds[k], :],
                        4 * part + k + side,
                        right if side else left,
                    )
                )
        end_copies.append(started(ends))
    middle_copies = started(
        [
            grad(gsend.at[side, :, thirds[1], :], grecv.at[1 - side, :, thirds[1], :], 8 + side, device)
            for side, device in enumerate((left, right))
        ]
    )

    middle_layer(3, a1, e1, a0, e0)

    keeps = (col > 0, col < 7)
    keeps_row = (tile_row > 0, tile_row < 15)

    def folded(part, k):
        total = acc[part, thirds[k], 128:256]
        for side in range(2):
            total = total + jnp.where(keeps[side], grecv[side, part, thirds[k], :].astype(F32), 0.0)
        return total

    row_copies = []
    for part in range(2):
        finished(end_copies[part])
        rsend[0, part] = folded(part, 0).astype(BF)
        rsend[1, part] = folded(part, 2).astype(BF)
        row_copies += started(
            [
                grad(rsend.at[0, part], rrecv.at[1, part], 10 + 2 * part, up),
                grad(rsend.at[1, part], rrecv.at[0, part], 11 + 2 * part, down),
            ]
        )

    middle_layer(4, a0, e0, a1, e1)

    middle_layer(5, a1, e1, a0, e0)

    for pair in range(STRIP // 2):
        y = dot_nt(t6b[...], window(a0, e0, pair, pair + 1))
        for r in range(2):
            for c in range(4):
                for k in range(2):
                    at_row = k * STRIP + 2 * pair + r
                    osc[c, at_row : at_row + 1, :] = y[r * 8 + c * 2 + k : r * 8 + c * 2 + k + 1, :]

    for half in range(2):
        joined = jnp.concatenate([osc[c, :, 128 * half : 128 * half + 128] for c in range(4)], axis=1)
        coarse = joined.astype(BF)
        fine = (joined - coarse.astype(F32)).astype(BF)
        both = dot(jnp.concatenate([coarse, fine], axis=0), p2[...])
        noise = both[0:32] + both[32:64]
        for k in range(2):
            cols = slice(512 * half, 512 * half + 512)
            reflect = xf[k, 8:24, cols] - 2.0 * noise[16 * k : 16 * k + 16]
            prior_out[k, :, cols] = 0.5 * xf[k, 8:24, cols] - 0.1 * reflect
            for c in range(4):
                prb[4 * half + c, k] = reflect[:, 128 * c : 128 * c + 128].astype(BF)
    pr_copies = []
    for k, c in enumerate(peers):
        pr_copies.append(remote(prb.at[c], prt.at[col], pr_send.at[k], pr_recv.at[k], (agent, row, c)))
        pr_copies[-1].start()
    prt[col] = prb[col]

    finished(middle_copies)
    for part in range(2):
        finished(row_copies[2 * part : 2 * part + 2])
        total = folded(part, 1)
        for side in range(2):
            total = total + jnp.where(keeps_row[side], rrecv[side, part].astype(F32), 0.0)
        reflect = ds_ref[part] - 0.25 * total
        acc[part, 128:256, 128:256] = reflect
        drb[part] = reflect.astype(BF)
    dr_copies = []
    for k, c in enumerate(peers):
        dr_copies.append(
            remote(
                drb.at[:, pl.ds(pl.multiple_of(c * STRIP, STRIP), STRIP), :],
                drs.at[col],
                dr_send.at[k],
                dr_recv.at[k],
                (agent, row, c),
            )
        )
        dr_copies[-1].start()
    drs[col] = drb[:, pl.ds(pl.multiple_of(col * STRIP, STRIP), STRIP), :]

    for copy in dr_copies:
        copy.wait()
    for c in range(8):
        cols = slice(128 * c, 128 * c + 128)
        for k in range(2):
            prior_out[k, :, cols] = prior_out[k, :, cols] + 0.6 * drs[c, k].astype(F32)
    store_prior = pltpu.make_async_copy(prior_out, prior_any, local_sem.at[8])
    store_prior.start()
    for copy in pr_copies:
        copy.wait()
    for c in range(8):
        rows = slice(STRIP * c, STRIP * c + STRIP)
        for k in range(2):
            data_out[k, rows, :] = (
                0.5 * ds_ref[k, rows, :]
                + 0.1 * acc[k, 128 + STRIP * c : 144 + STRIP * c, 128:256]
                + 0.4 * prt[c, k].astype(F32)
            )
    store_data = pltpu.make_async_copy(data_out, data_any, local_sem.at[9])
    store_data.start()
    store_prior.wait()
    store_data.wait()


def store(data_ref, prior_ref, data_any, prior_any, sems):
    copies = [
        pltpu.make_async_copy(source, target, sems.at[k])
        for k, (source, target) in enumerate(((data_ref, data_any), (prior_ref, prior_any)))
    ]
    for copy in copies:
        copy.start()
    for copy in copies:
        copy.wait()


def on_device(
    probe_field, offsets, amplitudes, data_state, prior_state, first_weights, middle_weights, last_weights
):
    hbm = pl.BlockSpec(memory_space=pltpu.HBM)
    vmem = pl.BlockSpec(memory_space=pltpu.VMEM)
    table = jnp.asarray(fourier_table()).astype(BF)
    dma = pltpu.SemaphoreType.DMA
    shapes = (
        jax.ShapeDtypeStruct((2, TILE, TILE), F32),
        jax.ShapeDtypeStruct((2, STRIP, 1024), F32),
    )
    results = pl.pallas_call(
        kernel,
        name="step",
        out_shape=shapes,
        in_specs=[
            pl.BlockSpec(memory_space=pltpu.SMEM),
            hbm,
            hbm,
            hbm,
            hbm,
            vmem,
            hbm,
            vmem,
            hbm,
        ],
        out_specs=(hbm, hbm),
        scratch_shapes=[
            pltpu.VMEM((2, TILE, TILE), F32),
            pltpu.VMEM((4, 3, 32, 96), BF),
            pltpu.VMEM((2, 256, 256), BF),
            pltpu.VMEM((2, TILE, TILE), F32),
            pltpu.VMEM((2, STRIP, 1024), F32),
            pltpu.VMEM((2, PROBE, PROBE), F32),
            pltpu.VMEM((POSITIONS, PROBE, PROBE), F32),
            pltpu.VMEM((2, 32, 1024), F32),
            pltpu.VMEM((2, 16, 1024), BF),
            pltpu.VMEM((2, 16, 1024), BF),
            pltpu.VMEM((2, EXT, TILE), BF),
            pltpu.VMEM((2, EXT, TILE), BF),
            pltpu.VMEM((2, EXT, TILE), BF),
            pltpu.VMEM((2, 2, EXT, TILE), BF),
            pltpu.VMEM((2, 2, EXT, TILE), BF),
            pltpu.VMEM((2, 2, TILE, TILE), BF),
            pltpu.VMEM((2, 2, TILE, TILE), BF),
            pltpu.VMEM((2, TILE, TILE), BF),
            pltpu.VMEM((8, 2, STRIP, TILE), BF),
            pltpu.VMEM((8, 2, STRIP, TILE), BF),
            pltpu.VMEM((8, 2, STRIP, TILE), BF),
            pltpu.VMEM((2, 3, EXT, TILE), F32),
            pltpu.VMEM((2, EXT, EXT), F32),
            pltpu.VMEM((512, 512), BF),
            pltpu.VMEM((512, 512), BF),
            pltpu.VMEM((1024, 512), BF),
            pltpu.VMEM((4, 512, 256), BF),
            pltpu.VMEM((4, 512, 256), F32),
            pltpu.VMEM((4, 2, 2, 512, 128), F32),
            pltpu.VMEM((128, 256), F32),
            pltpu.VMEM((4, 768, 256), BF),
            pltpu.VMEM((16, 768), F32),
            pltpu.VMEM((16, 768), BF),
            pltpu.VMEM((128, 512), BF),
            pltpu.VMEM((512, 512), BF),
            pltpu.VMEM((4, 128, 512), BF),
            pltpu.VMEM((2, 272, 128), F32),
            pltpu.VMEM((PAIRS, 256, 256), BF),
            pltpu.VMEM((PAIRS, 256, 256), BF),
            pltpu.VMEM((PAIRS, 256, 128), BF),
            pltpu.VMEM((PAIRS, 256, 128), BF),
            pltpu.VMEM((4, 272, 128), F32),
            pltpu.VMEM((4, 32, 256), F32),
            dma((10,)),
            dma((16,)),
            dma((16,)),
            dma((14,)),
            dma((14,)),
            dma((7,)),
            dma((7,)),
            dma((7,)),
            dma((7,)),
        ],
        compiler_params=pltpu.CompilerParams(
            collective_id=0, has_side_effects=True, vmem_limit_bytes=61 * 1024 * 1024
        ),
    )(
        offsets,
        probe_field,
        amplitudes.reshape(POSITIONS, PROBE, PROBE),
        data_state,
        prior_state,
        jnp.transpose(first_weights, (0, 2, 1)),
        middle_weights,
        last_weights,
        table,
    )
    return pl.pallas_call(
        store,
        name="store",
        out_shape=shapes,
        in_specs=[vmem, vmem],
        out_specs=(hbm, hbm),
        scratch_shapes=[dma((2,))],
    )(*results)


def solution(mesh):
    tiles = P(None, ("agent", "row"), "col")
    strips = P(None, ("agent", "row", "col"), None)
    in_specs = (P(), tiles, P(("agent", "row"), "col", None, None), tiles, strips, P(), P(), P())
    return jax.shard_map(
        on_device, mesh=mesh, in_specs=in_specs, out_specs=(tiles, strips), check_vma=False
    )
```

```python
import functools
import math

import jax
import jax.numpy as jnp
import numpy as np
from jax import lax
from jax.experimental import pallas as pl
from jax.experimental.pallas import tpu as pltpu
from jax.sharding import PartitionSpec as P

PROBE = 256
STEP = 64
JITTER = 32
TILE = 128
STRIP = 16
LAYERS = 6
EXT = 384
QUADS = 256
PAIRS = 13
POSITIONS = 4

BF = jnp.bfloat16
F32 = jnp.float32
MESH = pl.DeviceIdType.MESH


def fourier_table():
    numbers = np.arange(PROBE)
    product = (numbers[:, None] * numbers[None, :]) % PROBE
    angles = product * (2.0 * math.pi / PROBE)
    scaling = 1.0 / math.sqrt(PROBE)
    return np.stack([np.cos(angles) * scaling, -np.sin(angles) * scaling]).astype(np.float32)


def dot(left, right):
    return lax.dot_general(left, right, (((1,), (0,)), ((), ())), preferred_element_type=F32)


def dot_nt(left, right):
    return lax.dot_general(left, right, (((1,), (1,)), ((), ())), preferred_element_type=F32)


def slot_of(row, column):
    return column ^ 1 if row else column


def center_lane(row, column):
    return (row // 2) * 256 + (row % 2) * 128 + slot_of(row % 2, column) * 32


def edge_lane(row, column):
    odd = row % 2
    slot = (1 if odd else 0) if column == 4 else (2 if odd else 3)
    return 512 + (row // 2) * 128 + slot * 32


def input_lane(row, column):
    return center_lane(row, column) if 0 <= column < 4 else edge_lane(row, column)


def kernel(
    offsets,
    probe_any,
    amps_any,
    ds_any,
    ps_any,
    first_ref,
    middle_any,
    last_ref,
    table_any,
    data_any,
    prior_any,
    ds_ref,
    middle_ref,
    table_ref,
    data_out,
    prior_out,
    probe,
    amps,
    xf,
    hsend,
    hrecv,
    obh,
    obl,
    obr,
    gsend,
    grecv,
    rsend,
    rrecv,
    drb,
    drs,
    prb,
    prt,
    obj,
    acc,
    ff,
    gg,
    ex,
    hs,
    wave,
    cp,
    t1,
    tm,
    t6,
    t6b,
    d2,
    p2,
    xr,
    xv,
    a0,
    a1,
    e0,
    e1,
    zz,
    osc,
    local_sem,
    halo_send,
    halo_recv,
    grad_send,
    grad_recv,
    dr_send,
    dr_recv,
    pr_send,
    pr_recv,
):
    agent, row, col = lax.axis_index("agent"), lax.axis_index("row"), lax.axis_index("col")
    tile_row = agent * 8 + row
    strip = tile_row * 8 + col

    def at(tile, column):
        return (lax.div(tile, 8), lax.rem(tile, 8), column)

    up = at(lax.rem(tile_row + 15, 16), col)
    down = at(lax.rem(tile_row + 1, 16), col)
    left = (agent, row, lax.rem(col + 7, 8))
    right = (agent, row, lax.rem(col + 1, 8))
    before, after = lax.rem(strip + 127, 128), lax.rem(strip + 1, 128)
    prev_strip = at(lax.div(before, 8), lax.rem(before, 8))
    next_strip = at(lax.div(after, 8), lax.rem(after, 8))
    peers = [lax.rem(col + k, 8) for k in range(1, 8)]

    def remote(src, dst, send, recv, device):
        return pltpu.make_async_remote_copy(
            src_ref=src, dst_ref=dst, send_sem=send, recv_sem=recv, device_id=device, device_id_type=MESH
        )

    barrier = pltpu.get_barrier_semaphore()
    greeted = [up, down, prev_strip, next_strip] + [(agent, row, c) for c in peers]
    for device in greeted:
        pl.semaphore_signal(barrier, inc=1, device_id=device, device_id_type=MESH)
    loads = [
        pltpu.make_async_copy(source, target, local_sem.at[k])
        for k, (source, target) in enumerate(
            (
                (ds_any, ds_ref),
                (ps_any, xf.at[:, 8:24, :]),
                (middle_any, middle_ref),
                (table_any, table_ref),
                (probe_any, probe),
                (amps_any, amps),
            )
        )
    ]
    for load in loads:
        load.start()

    loads[0].wait()
    obh[:, 128:256, :] = ds_ref[...].astype(BF)
    pl.semaphore_wait(barrier, len(greeted))

    def started(copies):
        for copy in copies:
            copy.start()
        return copies

    def finished(copies):
        for copy in copies:
            copy.wait()

    def halo(src, dst, number, device):
        return remote(src, dst, halo_send.at[number], halo_recv.at[number], device)

    def grad(src, dst, number, device):
        return remote(src, dst, grad_send.at[number], grad_recv.at[number], device)

    thirds = [slice(128 * k, 128 * k + 128) for k in range(3)]
    row_halo = []
    for part in range(2):
        own = obh.at[part, thirds[1], :]
        row_halo.append(
            started(
                [
                    halo(own, obh.at[part, thirds[0], :], 2 + 2 * part, down),
                    halo(own, obh.at[part, thirds[2], :], 3 + 2 * part, up),
                ]
            )
        )
    col_halo = started(
        [
            halo(obh.at[:, thirds[1], :], obl.at[:, thirds[1], :], 6, right),
            halo(obh.at[:, thirds[1], :], obr.at[:, thirds[1], :], 7, left),
        ]
    )

    loads[1].wait()
    for side in range(2):
        rows = slice(8 + 8 * side, 16 + 8 * side)
        hsend[side] = jnp.concatenate([xf[0, rows, :], xf[1, rows, :]], axis=0).astype(BF)
    strip_halo = started(
        [
            halo(hsend.at[0], hrecv.at[1], 0, prev_strip),
            halo(hsend.at[1], hrecv.at[0], 1, next_strip),
        ]
    )

    for load in loads[2:4]:
        load.wait()
    t6[...] = jnp.zeros_like(t6)
    for r in range(2):
        for c in range(4):
            for a in range(3):
                for b in range(3):
                    lane = input_lane(r + a, c + b - 1)
                    t6[r * 8 + c * 2 : r * 8 + c * 2 + 2, lane : lane + 32] = last_ref[
                        a, :, 32 * b : 32 * b + 32
                    ].astype(F32)
    t6b[...] = t6[...].astype(BF)

    def banded(value_of, r, line, place, height):
        slots = lax.broadcasted_iota(jnp.int32, (height, 128), 1) // 32
        total = jnp.zeros((height, 128), F32)
        if 0 <= line - r <= 2:
            for b in range(3):
                c = place - b + 1
                if 0 <= c < 4:
                    total = jnp.where(slots == slot_of(r, c), value_of(line - r, b), total)
        return total

    for layer in range(4):
        turned = []
        for a in range(3):
            block = jnp.transpose(middle_ref[layer, a].astype(F32))
            turned.append(jnp.concatenate([block] * 4, axis=1))
        for line in range(4):
            for place in range(-1, 5):
                lane = input_lane(line, place)
                for r in range(2):
                    tm[layer, lane : lane + 32, 128 * r : 128 * r + 128] = banded(
                        lambda a, b: turned[a][32 * b : 32 * b + 32], r, line, place, 32
                    ).astype(BF)

    t1[...] = jnp.zeros_like(t1)
    firsts = [jnp.concatenate([first_ref[a].astype(F32)] * 4, axis=1) for a in range(3)]
    for line in range(4):
        for place in range(-1, 5):
            if 0 <= place < 4:
                lane = (place % 2) * 64 + 4 * (place // 2) + line
            else:
                lane = (0 if place == 4 else 64) + 8 + line
            for k in range(2):
                for r in range(2):
                    t1[lane + 32 * k : lane + 32 * k + 1, 128 * r : 128 * r + 128] = banded(
                        lambda a, b: firsts[a][2 * b + k : 2 * b + k + 1], r, line, place, 1
                    )

    vq = lax.broadcasted_iota(jnp.int32, (128, 512), 0)
    jc = lax.broadcasted_iota(jnp.int32, (128, 512), 1)
    hit = lax.rem(jc, 256) == 4 * lax.rem(vq, 64) + 2 * lax.div(vq, 64) + lax.div(jc, 256)
    d2[...] = jnp.where(hit, 1.0, 0.0).astype(BF)
    jq = lax.broadcasted_iota(jnp.int32, (512, 512), 0)
    cc = lax.broadcasted_iota(jnp.int32, (512, 512), 1)
    p2[...] = jnp.where(cc == 4 * lax.rem(jq, 128) + lax.div(jq, 128), 1.0, 0.0).astype(BF)

    real, imag = table_ref[0], table_ref[1]
    minus = (-imag.astype(F32)).astype(BF)
    ff[0:256, 0:256] = real
    ff[0:256, 256:512] = imag
    ff[256:512, 0:256] = minus
    ff[256:512, 256:512] = real
    gg[0:256, 0:256] = real
    gg[0:256, 256:512] = minus
    gg[256:512, 0:256] = imag
    gg[256:512, 256:512] = real

    for part in range(2):
        finished(row_halo[part])
        for k in (0, 2):
            rows = obh.at[part, thirds[k], :]
            number = 8 + 4 * part + 2 * (k // 2)
            col_halo += started(
                [
                    halo(rows, obl.at[part, thirds[k], :], number, right),
                    halo(rows, obr.at[part, thirds[k], :], number + 1, left),
                ]
            )

    finished(strip_halo)
    xr[...] = jnp.zeros_like(xr)
    zero_rows = jnp.zeros((8, 128), F32)
    for slot in range(2):
        xv[slot, 0:8, :] = zero_rows
        xv[slot, 264:272, :] = zero_rows
    for slot in range(4):
        zz[slot, 0:8, :] = zero_rows
        zz[slot, 264:272, :] = zero_rows
    keep_top = strip > 0
    keep_bottom = strip < 127
    for t in range(4):
        cols = slice(256 * t, 256 * t + 256)
        for k in range(2):
            piece = jnp.concatenate(
                [
                    jnp.where(keep_top, hrecv[0, 8 * k : 8 * k + 8, cols].astype(F32), 0.0),
                    xf[k, 8:24, cols],
                    jnp.where(keep_bottom, hrecv[1, 8 * k : 8 * k + 8, cols].astype(F32), 0.0),
                ],
                axis=0,
            ).astype(BF)
            xr[t, 32 * k : 32 * k + 32, 0:256] = piece
            xr[t, 64 + 32 * k : 96 + 32 * k, 256:512] = piece
        spread = dot_nt(d2[...], xr[t])
        xv[0, 8 + 64 * t : 72 + 64 * t, :] = spread[0:64]
        xv[1, 8 + 64 * t : 72 + 64 * t, :] = spread[64:128]
    wide_ids = lax.broadcasted_iota(jnp.int32, (QUADS, 128), 1)
    low_half = wide_ids < 64
    outer = (wide_ids < 32) | (wide_ids >= 96)

    def finish(y, first, pair, slot, a_out, e_out):
        top = first + 2 * pair
        in_top = (top >= 0) & (top < 2048)
        in_low = (top >= -1) & (top < 2047)
        y0 = jnp.where(in_top, jnp.maximum(y[:, 0:128], 0.0), 0.0)
        y1 = jnp.where(in_low, jnp.maximum(y[:, 128:256], 0.0), 0.0)
        a_out[pair, :, 0:128] = y0.astype(BF)
        a_out[pair, :, 128:256] = y1.astype(BF)
        zz[slot, 8:264, :] = jnp.where(outer, y0, y1)
        e_out[pair] = jnp.where(low_half, zz[slot, 9:265, :], zz[slot, 7:263, :]).astype(BF)

    base = strip * STRIP - LAYERS
    within = wide_ids & 31
    edges = jnp.where(low_half, xv[0, 9:265, :], xv[1, 7:263, :])

    def groups(count):
        parts = -(-count // 4)
        bounds = [count * k // parts for k in range(parts + 1)]
        return list(zip(bounds[:-1], bounds[1:]))

    for low, high in groups(PAIRS):
        taken = []
        for pair in range(low, high):
            shift = 128 - 2 - 2 * pair
            near = pltpu.roll(xv[0, 8:264, :], shift, 1)
            far = pltpu.roll(xv[1, 8:264, :], (shift + 4) % 128, 1)
            rest = pltpu.roll(edges, (shift + 8) % 128, 1)
            taken.append(jnp.where(within < 4, near, jnp.where(within < 8, far, rest)).astype(BF))
        y = dot(jnp.concatenate(taken, axis=0), t1[...].astype(BF))
        for pair in range(low, high):
            k = pair - low
            finish(y[256 * k : 256 * k + 256], base + 1, pair, k, a0, e0)

    def window(a_in, e_in, low, high):
        rows = (high - low) * QUADS
        parts = [
            a_in[low:high].reshape(rows, 256),
            a_in[low + 1 : high + 1].reshape(rows, 256),
            e_in[low:high].reshape(rows, 128),
            e_in[low + 1 : high + 1].reshape(rows, 128),
        ]
        return jnp.concatenate(parts, axis=1)

    def middle_layer(depth, a_in, e_in, a_out, e_out):
        for low, high in groups(PAIRS + 1 - depth):
            y = dot(window(a_in, e_in, low, high), tm[depth - 2])
            for pair in range(low, high):
                k = pair - low
                finish(y[256 * k : 256 * k + 256], base + depth, pair, k, a_out, e_out)

    middle_layer(2, a0, e0, a1, e1)

    def fill(block, third):
        column_in = (col > 0, True, col < 7)[block]
        inside = (tile_row > 0, True, tile_row < 15)[third]
        for part in range(2):
            if block == 1 and third == 1:
                value = ds_ref[part]
            else:
                source = (obl, obh, obr)[block]
                keep = jnp.logical_and(inside, column_in)
                value = jnp.where(keep, source[part, thirds[third], :].astype(F32), 0.0)
            obj[part, block, thirds[third], :] = value

    for third in range(3):
        fill(1, third)
    for number in range(POSITIONS):
        for part in range(2):
            for block in range(2):
                cp[number, part, block, 0:128, :] = jnp.zeros((128, 128), F32)
                cp[number, part, block, 384:512, :] = jnp.zeros((128, 128), F32)
    finished(loads[4:6])
    finished(col_halo)
    for block in (0, 2):
        for third in range(3):
            fill(block, third)

    places = []
    for number in range(POSITIONS):
        grid_row, grid_col = divmod(number, 2)
        places.append(
            (
                grid_row * STEP + JITTER + offsets[0, grid_row, grid_col],
                grid_col * STEP + JITTER + offsets[1, grid_row, grid_col],
            )
        )

    def transform(first, second):
        for number in range(0, POSITIONS, 2):
            rows = slice(256 * number, 256 * number + 512)
            for part in range(2):
                half = dot(ex[rows, :], first[:, 256 * part : 256 * part + 256]).astype(BF)
                for k in range(2):
                    hs[number + k, 256 * part : 256 * part + 256, :] = half[256 * k : 256 * k + 256]
        for number in range(POSITIONS):
            wave[number] = dot(second[...], hs[number])

    for number, (upper, lefty) in enumerate(places):
        back_roll = lax.rem(EXT - lefty, EXT)
        for chunk in range(0, PROBE, 64):
            rows = slice(chunk, chunk + 64)
            o_r, o_i = [
                pltpu.roll(
                    jnp.concatenate(
                        [obj[part, block, pl.ds(upper + chunk, 64), :] for block in range(3)], axis=1
                    ),
                    back_roll,
                    1,
                )[:, 0:256]
                for part in range(2)
            ]
            p_r, p_i = probe[0, rows, :], probe[1, rows, :]
            out = slice(256 * number + chunk, 256 * number + chunk + 64)
            ex[out, 0:256] = (p_r * o_r - p_i * o_i).astype(BF)
            ex[out, 256:512] = (p_r * o_i + p_i * o_r).astype(BF)
    transform(ff, gg)
    for number in range(POSITIONS):
        for chunk in range(0, PROBE, 64):
            rows = slice(chunk, chunk + 64)
            w_r, w_i = wave[number, rows, :], wave[number, 256 + chunk : 320 + chunk, :]
            square = w_r * w_r + w_i * w_i
            retained = 1.0 - amps[number, rows, :] * lax.rsqrt(jnp.maximum(square, 0.25))
            out = slice(256 * number + chunk, 256 * number + chunk + 64)
            ex[out, 0:256] = (w_r * retained).astype(BF)
            ex[out, 256:512] = (w_i * retained).astype(BF)
    transform(gg, ff)
    for number, (upper, lefty) in enumerate(places):
        for chunk in range(0, PROBE, 64):
            rows = slice(chunk, chunk + 64)
            f_r, f_i = wave[number, rows, :], wave[number, 256 + chunk : 320 + chunk, :]
            p_r, p_i = probe[0, rows, :], probe[1, rows, :]
            for part, term in enumerate((p_r * f_r + p_i * f_i, p_r * f_i - p_i * f_r)):
                for block in range(2):
                    cp[number, part, block, 128 + chunk : 192 + chunk, :] = term[
                        :, 128 * block : 128 * block + 128
                    ]
    end_copies = []
    for part in range(2):
        for chunk in range(0, EXT, 64):
            total = None
            for number, (upper, lefty) in enumerate(places):
                term = [cp[number, part, block, pl.ds(128 - upper + chunk, 64), :] for block in range(2)]
                term = jnp.concatenate(term + [jnp.zeros((64, 128), F32)], axis=1)
                term = pltpu.roll(term, lefty, 1)
                total = term if total is None else total + term
            acc[part, chunk : chunk + 64, :] = total
        gsend[0, part] = acc[part, :, 0:128].astype(BF)
        gsend[1, part] = acc[part, :, 256:384].astype(BF)
        ends = []
        for k in (0, 2):
            for side in range(2):
                ends.append(
                    grad(
                        gsend.at[side, part, thirds[k], :],
                        grecv.at[1 - side, part, thirds[k], :],
                        4 * part + k + side,
                        right if side else left,
                    )
                )
        end_copies.append(started(ends))
    middle_copies = started(
        [
            grad(gsend.at[side, :, thirds[1], :], grecv.at[1 - side, :, thirds[1], :], 8 + side, device)
            for side, device in enumerate((left, right))
        ]
    )

    middle_layer(3, a1, e1, a0, e0)

    keeps = (col > 0, col < 7)
    keeps_row = (tile_row > 0, tile_row < 15)

    def folded(part, k):
        total = acc[part, thirds[k], 128:256]
        for side in range(2):
            total = total + jnp.where(keeps[side], grecv[side, part, thirds[k], :].astype(F32), 0.0)
        return total

    row_copies = []
    for part in range(2):
        finished(end_copies[part])
        rsend[0, part] = folded(part, 0).astype(BF)
        rsend[1, part] = folded(part, 2).astype(BF)
        row_copies += started(
            [
                grad(rsend.at[0, part], rrecv.at[1, part], 10 + 2 * part, up),
                grad(rsend.at[1, part], rrecv.at[0, part], 11 + 2 * part, down),
            ]
        )

    middle_layer(4, a0, e0, a1, e1)

    middle_layer(5, a1, e1, a0, e0)

    for pair in range(STRIP // 2):
        y = dot_nt(t6b[...], window(a0, e0, pair, pair + 1))
        for r in range(2):
            for c in range(4):
                for k in range(2):
                    at_row = k * STRIP + 2 * pair + r
                    osc[c, at_row : at_row + 1, :] = y[r * 8 + c * 2 + k : r * 8 + c * 2 + k + 1, :]

    for half in range(2):
        joined = jnp.concatenate([osc[c, :, 128 * half : 128 * half + 128] for c in range(4)], axis=1)
        coarse = joined.astype(BF)
        fine = (joined - coarse.astype(F32)).astype(BF)
        both = dot(jnp.concatenate([coarse, fine], axis=0), p2[...])
        noise = both[0:32] + both[32:64]
        for k in range(2):
            cols = slice(512 * half, 512 * half + 512)
            reflect = xf[k, 8:24, cols] - 2.0 * noise[16 * k : 16 * k + 16]
            prior_out[k, :, cols] = 0.5 * xf[k, 8:24, cols] - 0.1 * reflect
            for c in range(4):
                prb[4 * half + c, k] = reflect[:, 128 * c : 128 * c + 128].astype(BF)
    pr_copies = []
    for k, c in enumerate(peers):
        pr_copies.append(remote(prb.at[c], prt.at[col], pr_send.at[k], pr_recv.at[k], (agent, row, c)))
        pr_copies[-1].start()
    prt[col] = prb[col]

    finished(middle_copies)
    for part in range(2):
        finished(row_copies[2 * part : 2 * part + 2])
        total = folded(part, 1)
        for side in range(2):
            total = total + jnp.where(keeps_row[side], rrecv[side, part].astype(F32), 0.0)
        reflect = ds_ref[part] - 0.25 * total
        acc[part, 128:256, 128:256] = reflect
        drb[part] = reflect.astype(BF)
    dr_copies = []
    for k, c in enumerate(peers):
        dr_copies.append(
            remote(
                drb.at[:, pl.ds(pl.multiple_of(c * STRIP, STRIP), STRIP), :],
                drs.at[col],
                dr_send.at[k],
                dr_recv.at[k],
                (agent, row, c),
            )
        )
        dr_copies[-1].start()
    drs[col] = drb[:, pl.ds(pl.multiple_of(col * STRIP, STRIP), STRIP), :]

    for copy in dr_copies:
        copy.wait()
    for c in range(8):
        cols = slice(128 * c, 128 * c + 128)
        for k in range(2):
            prior_out[k, :, cols] = prior_out[k, :, cols] + 0.6 * drs[c, k].astype(F32)
    store_prior = pltpu.make_async_copy(prior_out, prior_any, local_sem.at[8])
    store_prior.start()
    for copy in pr_copies:
        copy.wait()
    for c in range(8):
        rows = slice(STRIP * c, STRIP * c + STRIP)
        for k in range(2):
            data_out[k, rows, :] = (
                0.5 * ds_ref[k, rows, :]
                + 0.1 * acc[k, 128 + STRIP * c : 144 + STRIP * c, 128:256]
                + 0.4 * prt[c, k].astype(F32)
            )
    store_data = pltpu.make_async_copy(data_out, data_any, local_sem.at[9])
    store_data.start()
    store_prior.wait()
    store_data.wait()


def store(data_ref, prior_ref, data_any, prior_any, sems):
    copies = [
        pltpu.make_async_copy(source, target, sems.at[k])
        for k, (source, target) in enumerate(((data_ref, data_any), (prior_ref, prior_any)))
    ]
    for copy in copies:
        copy.start()
    for copy in copies:
        copy.wait()


def on_device(
    probe_field, offsets, amplitudes, data_state, prior_state, first_weights, middle_weights, last_weights
):
    hbm = pl.BlockSpec(memory_space=pltpu.HBM)
    vmem = pl.BlockSpec(memory_space=pltpu.VMEM)
    table = jnp.asarray(fourier_table()).astype(BF)
    dma = pltpu.SemaphoreType.DMA
    shapes = (
        jax.ShapeDtypeStruct((2, TILE, TILE), F32),
        jax.ShapeDtypeStruct((2, STRIP, 1024), F32),
    )
    results = pl.pallas_call(
        kernel,
        name="step",
        out_shape=shapes,
        in_specs=[
            pl.BlockSpec(memory_space=pltpu.SMEM),
            hbm,
            hbm,
            hbm,
            hbm,
            vmem,
            hbm,
            vmem,
            hbm,
        ],
        out_specs=(hbm, hbm),
        scratch_shapes=[
            pltpu.VMEM((2, TILE, TILE), F32),
            pltpu.VMEM((4, 3, 32, 96), BF),
            pltpu.VMEM((2, 256, 256), BF),
            pltpu.VMEM((2, TILE, TILE), F32),
            pltpu.VMEM((2, STRIP, 1024), F32),
            pltpu.VMEM((2, PROBE, PROBE), F32),
            pltpu.VMEM((POSITIONS, PROBE, PROBE), F32),
            pltpu.VMEM((2, 32, 1024), F32),
            pltpu.VMEM((2, 16, 1024), BF),
            pltpu.VMEM((2, 16, 1024), BF),
            pltpu.VMEM((2, EXT, TILE), BF),
            pltpu.VMEM((2, EXT, TILE), BF),
            pltpu.VMEM((2, EXT, TILE), BF),
            pltpu.VMEM((2, 2, EXT, TILE), BF),
            pltpu.VMEM((2, 2, EXT, TILE), BF),
            pltpu.VMEM((2, 2, TILE, TILE), BF),
            pltpu.VMEM((2, 2, TILE, TILE), BF),
            pltpu.VMEM((2, TILE, TILE), BF),
            pltpu.VMEM((8, 2, STRIP, TILE), BF),
            pltpu.VMEM((8, 2, STRIP, TILE), BF),
            pltpu.VMEM((8, 2, STRIP, TILE), BF),
            pltpu.VMEM((2, 3, EXT, TILE), F32),
            pltpu.VMEM((2, EXT, EXT), F32),
            pltpu.VMEM((512, 512), BF),
            pltpu.VMEM((512, 512), BF),
            pltpu.VMEM((1024, 512), BF),
            pltpu.VMEM((4, 512, 256), BF),
            pltpu.VMEM((4, 512, 256), F32),
            pltpu.VMEM((4, 2, 2, 512, 128), F32),
            pltpu.VMEM((128, 256), F32),
            pltpu.VMEM((4, 768, 256), BF),
            pltpu.VMEM((16, 768), F32),
            pltpu.VMEM((16, 768), BF),
            pltpu.VMEM((128, 512), BF),
            pltpu.VMEM((512, 512), BF),
            pltpu.VMEM((4, 128, 512), BF),
            pltpu.VMEM((2, 272, 128), F32),
            pltpu.VMEM((PAIRS, 256, 256), BF),
            pltpu.VMEM((PAIRS, 256, 256), BF),
            pltpu.VMEM((PAIRS, 256, 128), BF),
            pltpu.VMEM((PAIRS, 256, 128), BF),
            pltpu.VMEM((4, 272, 128), F32),
            pltpu.VMEM((4, 32, 256), F32),
            dma((10,)),
            dma((16,)),
            dma((16,)),
            dma((14,)),
            dma((14,)),
            dma((7,)),
            dma((7,)),
            dma((7,)),
            dma((7,)),
        ],
        compiler_params=pltpu.CompilerParams(
            collective_id=0, has_side_effects=True, vmem_limit_bytes=61 * 1024 * 1024
        ),
    )(
        offsets,
        probe_field,
        amplitudes.reshape(POSITIONS, PROBE, PROBE),
        data_state,
        prior_state,
        jnp.transpose(first_weights, (0, 2, 1)),
        middle_weights,
        last_weights,
        table,
    )
    return pl.pallas_call(
        store,
        name="store",
        out_shape=shapes,
        in_specs=[vmem, vmem],
        out_specs=(hbm, hbm),
        scratch_shapes=[dma((2,))],
    )(*results)


def solution(mesh):
    tiles = P(None, ("agent", "row"), "col")
    strips = P(None, ("agent", "row", "col"), None)
    in_specs = (P(), tiles, P(("agent", "row"), "col", None, None), tiles, strips, P(), P(), P())
    return jax.shard_map(
        on_device, mesh=mesh, in_specs=in_specs, out_specs=(tiles, strips), check_vma=False
    )
```
